32 devices in a mesh: gx: 8 (over z, x), gy: 4 (over y, core).
Axes of the slice: x: 2, y: 2, z: 4, core: 2. Of those that a mesh axis runs over, the one named last changes fastest.
Arguments:
- object_field: float32 [2, 2048, 1024], P(None, 'gx', 'gy'), may hold values from -4.5 to 4.5
- probe_field: float32 [2, 2, 256, 256], replicated, may hold values from -4.2 to 4.2
- amplitude: float32 [32, 4, 256, 256], P('gx', 'gy'), may hold values from 0.2 to 3
- offsets: int32 [32, 4, 2], P('gx', 'gy'), may hold values from -128 to 128
Outputs:
- updated_object: float32 [2, 2048, 1024], P(None, 'gx', 'gy')
- updated_probe: float32 [2, 2, 256, 256], replicated
The draws below stay inside these ranges and needn't reach their ends.
All inputs are finite; a program needn't handle non-finite values.
Results may differ from the reference program's by a relative error of at most 0.0006.
The reference program's roundings to bfloat16 on the way count: a program that leaves them out, or rounds other values in their place, can miss the bound.
Values sent between devices are 32-bit elements; how exact they have to be, the bound alone decides.
A program may use at most 64 MiB of HBM per device.

```python
import math
import jax
import jax.numpy as jnp
from jax import lax

W = 256
MODES = 2
TILE = 256
POS = 4
NR = 2048
NC = 1024
N_GX = 8
N_GY = 4


def draw_object_field(key, part):
    key_mag = jax.random.fold_in(key, 11)
    key_phase = jax.random.fold_in(key, 12)
    rows = jnp.arange(NR, dtype=jnp.float32)[:, None] / NR
    cols = jnp.arange(NC, dtype=jnp.float32)[None, :] / NC
    ramp = jnp.sqrt((1.0 + 2.0 * rows) * (1.0 + 2.0 * cols)) / 1.7
    rough = jax.random.uniform(key_mag, (NR, NC), jnp.float32, 0.5, 1.2)
    angles = jax.random.uniform(key_phase, (NR, NC), jnp.float32, -math.pi, math.pi)
    magnitude = rough * ramp
    return jnp.stack([magnitude * jnp.cos(angles), magnitude * jnp.sin(angles)], 0)


def touch_ends(entries, key, smallest, high):
    longest = entries.shape.index(max(entries.shape))
    spots = []
    for shift in (0, 1):
        where = [jax.random.randint(jax.random.fold_in(key, axis), (), 0, length) for axis, length in enumerate(entries.shape)]
        where[longest] = (where[longest] + shift) % entries.shape[longest]
        spots.append(tuple(where))
    return entries.at[spots[0]].set(smallest).at[spots[1]].set(high)


def levels(rng, dims, split, smallest, largest):
    level = 1.0
    for axis_at, shards_of in split:
        draws = jax.random.uniform(jax.random.fold_in(jax.random.fold_in(rng, 6), axis_at), (shards_of,), jnp.float32, smallest / len(split), largest / len(split))
        level = level * jnp.repeat(jnp.exp(draws), dims[axis_at] // shards_of).reshape((-1,) + (1,) * (len(dims) - 1 - axis_at))
    return level


def scatter_about(key, dims, scale, most, kind=jnp.bfloat16):
    entries = scale * jax.random.normal(key, dims, jnp.float32)
    return jnp.clip(entries, min=-most, max=most).astype(kind)


def setup_inputs(seed: int = 0) -> dict:
    keys = jax.random.split(jax.random.key(seed), 5)
    object_field = draw_object_field(jax.random.fold_in(keys[4], 71), 0)
    probe_field = scatter_about(keys[1], (MODES, 2, W, W), 0.7, 4.2, jnp.float32)
    amplitude = jnp.clip(jnp.exp(math.log(3.0) - 2.7080502 * jax.random.uniform(keys[2], (POS * N_GX, N_GY, W, W), jnp.float32) ** levels(keys[2], (POS * N_GX, N_GY, W, W), ((0, 8), (1, 4)), -0.2, 0.2)), 0.2, 3.0)
    offsets = touch_ends(jax.random.randint(keys[3], (POS * N_GX, N_GY, 2), 0 - W // 2, TILE - W // 2 + 1), jax.random.fold_in(keys[3], 1), 0 - W // 2, (TILE - W // 2 + 1) - 1).astype(jnp.int32)
    return {"object_field": object_field, "probe_field": probe_field, "amplitude": amplitude, "offsets": offsets}


def dft_tables(extent):
    indices = jnp.arange(extent, dtype=jnp.int32)
    phases = indices[:, None] * indices[None, :] % extent
    angles = phases.astype(jnp.float32) * (2.0 * math.pi / extent)
    norm_factor = 1.0 / math.sqrt(extent)
    return ((jnp.cos(angles) * norm_factor).astype(jnp.bfloat16), (jnp.sin(angles) * norm_factor).astype(jnp.bfloat16))

def to_half(values):
    return lax.optimization_barrier(values.astype(jnp.bfloat16)).astype(jnp.float32)

def row_pass(cosine, sine, real_part, imag_part, orient):
    amount = real_part.shape[0]
    stacked = jnp.concatenate([real_part, imag_part], 0).astype(jnp.float32)
    with_cos = jnp.einsum('jk,bkl->bjl', cosine.astype(jnp.float32), stacked)
    with_sin = jnp.einsum('jk,bkl->bjl', sine.astype(jnp.float32), stacked)
    return (with_cos[:amount] + orient * with_sin[amount:], with_cos[amount:] - orient * with_sin[:amount])

def col_pass(cosine, sine, real_part, imag_part, orient):
    amount = real_part.shape[0]
    stacked = jnp.concatenate([real_part, imag_part], 0).astype(jnp.float32)
    with_cos = jnp.einsum('bjk,kl->bjl', stacked, cosine.astype(jnp.float32))
    with_sin = jnp.einsum('bjk,kl->bjl', stacked, sine.astype(jnp.float32))
    return (with_cos[:amount] + orient * with_sin[amount:], with_cos[amount:] - orient * with_sin[:amount])

def corrections(windows, probe_field, amplitude, cosine, sine):
    extent = probe_field.shape[-1]
    obj_real = windows[:, None, 0]
    obj_imag = windows[:, None, 1]
    probe_real = probe_field[None, :, 0]
    probe_imag = probe_field[None, :, 1]
    psi_real = probe_real * obj_real - probe_imag * obj_imag
    psi_imag = probe_real * obj_imag + probe_imag * obj_real
    amount = psi_real.shape[0]
    mode_count = psi_real.shape[1]
    shape_flat = (amount * mode_count, extent, extent)
    shape_full = (amount, mode_count, extent, extent)
    rows_real, rows_imag = row_pass(cosine, sine, to_half(psi_real.reshape(shape_flat)), to_half(psi_imag.reshape(shape_flat)), 1.0)
    far_real, far_imag = col_pass(cosine, sine, to_half(rows_real), to_half(rows_imag), 1.0)
    far_real = far_real.reshape(shape_full)
    far_imag = far_imag.reshape(shape_full)
    intensity = lax.optimization_barrier(jnp.sum(far_real * far_real + far_imag * far_imag, axis=1))
    factor = (amplitude / jnp.maximum(jnp.sqrt(intensity), 0.25))[:, None]
    proj_real = to_half((far_real * factor).reshape(shape_flat))
    proj_imag = to_half((far_imag * factor).reshape(shape_flat))
    back_rows_real, back_rows_imag = row_pass(cosine, sine, proj_real, proj_imag, -1.0)
    back_real, back_imag = col_pass(cosine, sine, to_half(back_rows_real), to_half(back_rows_imag), -1.0)
    diff_real = back_real.reshape(shape_full) - psi_real
    diff_imag = back_imag.reshape(shape_full) - psi_imag
    object_real = lax.optimization_barrier(jnp.sum(probe_real * diff_real + probe_imag * diff_imag, axis=1))
    object_imag = lax.optimization_barrier(jnp.sum(probe_real * diff_imag - probe_imag * diff_real, axis=1))
    grad_real = lax.optimization_barrier(jnp.sum(obj_real * diff_real + obj_imag * diff_imag, axis=0))
    grad_imag = lax.optimization_barrier(jnp.sum(obj_real * diff_imag - obj_imag * diff_real, axis=0))
    weight = lax.optimization_barrier(jnp.sum(windows[:, 0] * windows[:, 0] + windows[:, 1] * windows[:, 1], axis=0))
    return (jnp.stack([object_real, object_imag], 1), grad_real, grad_imag, weight)

def reference(object_field, probe_field, amplitude, offsets):
    extent = probe_field.shape[-1]
    margin = extent // 2
    mode_count = probe_field.shape[0]
    cosine, sine = dft_tables(extent)
    padded = jnp.pad(object_field, ((0, 0), (margin, margin), (margin, margin)), mode='wrap')
    zero_index = jnp.zeros((), jnp.int32)

    def tile_step(running, tile_number):
        accum, grad_real, grad_imag, weight = running
        tile_row = tile_number // N_GY
        tile_col = tile_number % N_GY
        tile_offsets = lax.dynamic_slice(offsets, (tile_row * POS, tile_col, zero_index), (POS, 1, 2))[:, 0]
        tile_amp = lax.dynamic_slice(amplitude, (tile_row * POS, tile_col, zero_index, zero_index), (POS, 1, extent, extent))[:, 0]
        row_starts = (tile_row * TILE + tile_offsets[:, 0] + margin).astype(jnp.int32)
        col_starts = (tile_col * TILE + tile_offsets[:, 1] + margin).astype(jnp.int32)
        windows = jnp.stack([lax.dynamic_slice(padded, (zero_index, row_starts[position], col_starts[position]), (2, extent, extent)) for position in range(POS)], 0)
        terms, step_real, step_imag, step_weight = corrections(windows, probe_field, tile_amp, cosine, sine)
        for position in range(POS):
            where = (zero_index, row_starts[position], col_starts[position])
            current = lax.dynamic_slice(accum, where, (2, extent, extent))
            accum = lax.dynamic_update_slice(accum, current + terms[position], where)
        return ((accum, grad_real + step_real, grad_imag + step_imag, weight + step_weight), None)
    start_state = (jnp.zeros((2, NR + 2 * margin, NC + 2 * margin), jnp.float32), jnp.zeros((mode_count, extent, extent), jnp.float32), jnp.zeros((mode_count, extent, extent), jnp.float32), jnp.zeros((extent, extent), jnp.float32))
    final_state, _ = lax.scan(tile_step, start_state, jnp.arange(N_GX * N_GY, dtype=jnp.int32))
    accum, grad_real, grad_imag, weight = final_state
    cols_core = accum[:, :, margin:margin + NC]
    cols_core = cols_core.at[:, :, NC - margin:].add(accum[:, :, :margin])
    cols_core = cols_core.at[:, :, :margin].add(accum[:, :, NC + margin:])
    object_step = cols_core[:, margin:margin + NR]
    object_step = object_step.at[:, NR - margin:].add(cols_core[:, :margin])
    object_step = object_step.at[:, :margin].add(cols_core[:, NR + margin:])
    updated_probe = probe_field + jnp.stack([grad_real, grad_imag], 1) / (weight + 1e-05)
    power = lax.optimization_barrier(jnp.sum(probe_field * probe_field, axis=(0, 1)))
    scale_max = jnp.max(power) + 1e-06
    updated_object = object_field + object_step / scale_max
    return (updated_object, updated_probe)
```

```python
import functools
import math

import jax
import jax.numpy as jnp
import numpy as np
from jax import lax
from jax.experimental import pallas as pl
from jax.experimental.pallas import tpu as pltpu
from jax.sharding import PartitionSpec as P

MESH = pl.DeviceIdType.MESH
VMEM = pl.BlockSpec(memory_space=pltpu.VMEM)
ANY = pl.BlockSpec(memory_space=pl.ANY)
F32 = jnp.float32
BF16 = jnp.bfloat16
CHUNK = 32
SUB = 8
STRIPS = 4
PIECES = 8
MIDS = 4
LIMIT = 30 << 20


def dft_tables(extent):
    indices = np.arange(extent)
    angles = (indices[:, None] * indices[None, :] % extent) * (2.0 * math.pi / extent)
    norm_factor = 1.0 / math.sqrt(extent)
    both = np.concatenate([np.cos(angles), np.sin(angles)], 1) * norm_factor
    return jnp.asarray(both.astype(np.float32).astype(jnp.bfloat16))


def remote(src, dst, sems, slot, device):
    return pltpu.make_async_remote_copy(
        src_ref=src,
        dst_ref=dst,
        send_sem=sems.at[0, slot],
        recv_sem=sems.at[1, slot],
        device_id=device,
        device_id_type=MESH,
    )


def greet(devices):
    barrier = pltpu.get_barrier_semaphore()
    for device in devices:
        pl.semaphore_signal(barrier, inc=1, device_id=device, device_id_type=MESH)
    pl.semaphore_wait(barrier, len(devices))


def halo_kernel(n_gx, n_gy, margin, obj, ext, sems, local_sem):
    gx, gy = lax.axis_index("gx"), lax.axis_index("gy")
    rows, cols = obj.shape[1], obj.shape[2]
    m = margin
    up = (lax.rem(gx + n_gx - 1, n_gx), gy)
    down = (lax.rem(gx + 1, n_gx), gy)
    left = (gx, lax.rem(gy + n_gy - 1, n_gy))
    right = (gx, lax.rem(gy + 1, n_gy))
    own = pltpu.make_async_copy(
        obj, ext.at[:, pl.ds(m, rows), pl.ds(m, cols)], local_sem.at[0]
    )
    own.start()
    greet((up, down, left, right))
    lcol, rcol = pl.ds(0, m), pl.ds(m + cols, m)
    mid_r, mid_c = pl.ds(m, rows), pl.ds(m, cols)
    piece = m // STRIPS
    slot = [0]

    def send(src, dst, device):
        copy = remote(src, dst, sems, slot[0], device)
        slot[0] += 1
        copy.start()
        return copy

    vertical = []
    for i in range(STRIPS):
        at = i * piece
        for src, dst, device in ((rows - m + at, at, down), (at, m + rows + at, up)):
            band = pl.ds(dst, piece)
            copy = send(obj.at[:, pl.ds(src, piece), :], ext.at[:, band, mid_c], device)
            vertical.append((copy, band))
    pending = [
        send(obj.at[:, :, pl.ds(cols - m, m)], ext.at[:, mid_r, lcol], right),
        send(obj.at[:, :, pl.ds(0, m)], ext.at[:, mid_r, rcol], left),
    ]
    for copy, band in vertical:
        copy.wait_recv()
        pending.append(send(ext.at[:, band, pl.ds(cols, m)], ext.at[:, band, lcol], right))
        pending.append(send(ext.at[:, band, pl.ds(m, m)], ext.at[:, band, rcol], left))
    for copy in pending:
        copy.wait_recv()
    for copy in pending:
        copy.wait_send()
    for copy, _ in vertical:
        copy.wait_send()
    own.wait()


def update_kernel(
    margin, offs, ext, probe, amp, table, acc, sums, win, psi, xbuf, ybuf, far, fr, frt
):
    p = pl.program_id(0)
    extent = probe.shape[-1]
    modes = probe.shape[0]
    width = ext.shape[2]
    r0 = offs[0, 0, p] + margin
    c0 = offs[0, 1, p] + margin
    back_shift = lax.rem(width - c0, width)
    low = lax.rem(r0, SUB)
    base = r0 - low
    tall = CHUNK + SUB
    row_shift = lax.rem(tall - low, tall)
    n_chunks = extent // CHUNK

    @pl.when(p == 0)
    def _():
        acc[...] = jnp.zeros_like(acc)
        sums[...] = jnp.zeros_like(sums)
        c, s = table[:, :extent], table[:, extent:]
        fr[:extent, :extent] = c
        fr[:extent, extent:] = s
        fr[extent:, :extent] = -s
        fr[extent:, extent:] = c
        frt[:extent, :extent] = c
        frt[:extent, extent:] = -s
        frt[extent:, :extent] = s
        frt[extent:, extent:] = c

    @pl.loop(0, n_chunks, unroll=8)
    def _(i):
        rb = pl.multiple_of(i * CHUNK, CHUNK)
        here = pl.ds(rb, CHUNK)
        w = []
        for part in range(2):
            line = ext[part, pl.ds(pl.multiple_of(base + rb, SUB), tall), :]
            line = pltpu.roll(line, row_shift, 0)[:CHUNK]
            w.append(pltpu.roll(line, back_shift, 1)[:, :extent])
            win[part, here, :] = w[part]
        sums[2 * modes, here, :] += w[0] * w[0] + w[1] * w[1]
        for k in range(modes):
            cols = slice(k * extent, (k + 1) * extent)
            pr, pi = probe[k, 0, here, :], probe[k, 1, here, :]
            psi_re = pr * w[0] - pi * w[1]
            psi_im = pr * w[1] + pi * w[0]
            psi[k, 0, here, :] = psi_re
            psi[k, 1, here, :] = psi_im
            xbuf[here, cols] = psi_re.astype(BF16)
            xbuf[pl.ds(extent + rb, CHUNK), cols] = psi_im.astype(BF16)

    def rows_then_cols(row_table, col_table):
        for part in range(2):
            table = row_table[part * extent : (part + 1) * extent, :]
            out = jnp.dot(table, xbuf[...], preferred_element_type=F32).astype(BF16)
            for k in range(modes):
                ybuf[k * extent : (k + 1) * extent, part * extent : (part + 1) * extent] = out[
                    :, k * extent : (k + 1) * extent
                ]
        for k in range(modes):
            band = slice(k * extent, (k + 1) * extent)
            far[band, :] = jnp.dot(ybuf[band, :], col_table[...], preferred_element_type=F32)

    rows_then_cols(fr, frt)

    @pl.loop(0, n_chunks, unroll=8)
    def _(i):
        rb = pl.multiple_of(i * CHUNK, CHUNK)
        parts = []
        intensity = jnp.zeros((CHUNK, extent), F32)
        for k in range(modes):
            at = pl.ds(k * extent + rb, CHUNK)
            re, im = far[at, :extent], far[at, extent:]
            intensity += re * re + im * im
            parts.append((re, im))
        factor = amp[0, pl.ds(rb, CHUNK), :] * jnp.minimum(lax.rsqrt(intensity), 4.0)
        for k in range(modes):
            cols = slice(k * extent, (k + 1) * extent)
            xbuf[pl.ds(rb, CHUNK), cols] = (parts[k][0] * factor).astype(BF16)
            xbuf[pl.ds(extent + rb, CHUNK), cols] = (parts[k][1] * factor).astype(BF16)

    rows_then_cols(frt, fr)

    @pl.loop(0, n_chunks, unroll=8)
    def _(i):
        rb = pl.multiple_of(i * CHUNK, CHUNK)
        here = pl.ds(rb, CHUNK)
        wr, wi = win[0, here, :], win[1, here, :]
        obj_re = jnp.zeros((CHUNK, extent), F32)
        obj_im = jnp.zeros((CHUNK, extent), F32)
        for k in range(modes):
            at = pl.ds(k * extent + rb, CHUNK)
            dr = far[at, :extent] - psi[k, 0, here, :]
            di = far[at, extent:] - psi[k, 1, here, :]
            pr, pi = probe[k, 0, here, :], probe[k, 1, here, :]
            obj_re += pr * dr + pi * di
            obj_im += pr * di - pi * dr
            sums[2 * k, here, :] += wr * dr + wi * di
            sums[2 * k + 1, here, :] += wr * di - wi * dr
        blank = jnp.zeros((CHUNK, width - extent), F32)
        below = jnp.zeros((SUB, width), F32)
        for part, value in enumerate((obj_re, obj_im)):
            line = pltpu.roll(jnp.concatenate([value, blank], 1), lax.rem(c0, width), 1)
            line = pltpu.roll(jnp.concatenate([line, below], 0), low, 0)
            acc[part, pl.ds(pl.multiple_of(base + rb, SUB), tall), :] += line


def reduce_plan(n_gx, n_gy):
    x_bits, y_bits = n_gx.bit_length() - 1, n_gy.bit_length() - 1
    core, x, y = ("gy", 0, 1), ("gx", 0, 1), ("gy", 1, 1)
    z = ("gx", 1, min(2, x_bits - 1))
    rest = [("gx", b, 1) for b in range(3, x_bits)] + [("gy", b, 1) for b in range(2, y_bits)]
    return ([core, x, y, z] + rest, [core, y, x, z] + rest)


def fold_kernel(n_gx, n_gy, margin, acc, obj, probe, sums, out_obj, out_probe, *scratch):
    (from_left, from_right, send_up, send_down, from_up, from_down, part, inbox, sems) = scratch
    gx, gy = lax.axis_index("gx"), lax.axis_index("gy")
    rows, cols = obj.shape[1], obj.shape[2]
    planes, extent = sums.shape[0], sums.shape[1]
    modes = probe.shape[0]
    m = margin
    up = (lax.rem(gx + n_gx - 1, n_gx), gy)
    down = (lax.rem(gx + 1, n_gx), gy)
    left = (gx, lax.rem(gy + n_gy - 1, n_gy))
    right = (gx, lax.rem(gy + 1, n_gy))
    plan = reduce_plan(n_gx, n_gy)

    def members(axis, bit, count):
        size, step = 1 << count, 1 << bit
        coord = gx if axis == "gx" else gy
        mine = lax.rem(coord // step, size)
        peers = []
        for d in range(1, size):
            field = lax.rem(mine + d, size)
            other = coord + step * (field - mine)
            peers.append((field, (other, gy) if axis == "gx" else (gx, other)))
        return size, mine, peers

    greet([up, down, left, right] + [dev for g in plan[0] for _, dev in members(*g)[2]])

    slot = [0]
    pending = []

    def send(src, dst, device):
        copy = remote(src, dst, sems, slot[0], device)
        slot[0] += 1
        copy.start()
        pending.append(copy)
        return copy

    lcol, rcol = pl.ds(0, m), pl.ds(m + cols, m)
    bands = (pl.ds(0, m), pl.ds(m + rows, m))
    mid = pl.ds(m, rows)

    def strip(band):
        return (
            send(acc.at[:, band, lcol], from_right.at[:, band, :], left),
            send(acc.at[:, band, rcol], from_left.at[:, band, :], right),
        )

    lanes = len(plan)
    lane_w = extent // lanes
    state = [{"off": 0, "n": extent, "src": sums, "box": 0} for _ in range(lanes)]
    history = [[] for _ in range(lanes)]

    def reduce_start(step):
        started = []
        for lane in range(lanes):
            s = state[lane]
            size, mine, peers = members(*plan[lane][step])
            at = pl.ds(lane * lane_w, lane_w)
            split = s["n"] % (size * SUB) == 0
            n = s["n"] // size if split else s["n"]
            copies = []
            for field, device in peers:
                give = s["off"] + field * n if split else s["off"]
                src = s["src"].at[:, pl.ds(pl.multiple_of(give, SUB), n), at]
                box = inbox.at[:, pl.ds(pl.multiple_of(s["box"] + mine * n, SUB), n), at]
                copies.append(send(src, box, device))
            keep = s["off"] + mine * n if split else s["off"]
            history[lane].append((size, mine, peers, split))
            started.append((copies, keep, n, size, mine, s["box"]))
            s["box"] += size * n
        return started

    def reduce_end(step, started):
        for lane, (copies, keep, n, size, mine, box) in enumerate(started):
            s = state[lane]
            at = pl.ds(lane * lane_w, lane_w)
            own = s["src"][:, pl.ds(pl.multiple_of(keep, SUB), n), at]
            inbox[:, pl.ds(pl.multiple_of(box + mine * n, SUB), n), at] = own
            for copy in copies:
                copy.wait_recv()
            total = inbox[:, pl.ds(box, n), at]
            for j in range(1, size):
                total += inbox[:, pl.ds(box + j * n, n), at]
            part[step, :, pl.ds(pl.multiple_of(keep, SUB), n), at] = total
            s["off"], s["n"], s["src"] = keep, n, part.at[step]

    def fold_band(copies, band, buf):
        for copy in copies:
            copy.wait_recv()
        buf[:, :, :m] = acc[:, band, pl.ds(m, m)] + from_left[:, band, :]
        if cols > 2 * m:
            buf[:, :, m : cols - m] = acc[:, band, pl.ds(2 * m, cols - 2 * m)]
        buf[:, :, cols - m :] = acc[:, band, pl.ds(cols, m)] + from_right[:, band, :]

    piece = m // PIECES
    folded = []

    def vertical(ups, downs):
        for i in ups:
            at = pl.ds(i * piece, piece)
            folded.append(send(send_up.at[:, at, :], from_down.at[:, at, :], up))
        for i in downs:
            at = pl.ds(i * piece, piece)
            folded.append(send(send_down.at[:, at, :], from_up.at[:, at, :], down))

    def middle(i):
        folded.extend(strip(pl.ds(m + i * (rows // MIDS), rows // MIDS)))

    started = reduce_start(0)
    corner_up = strip(bands[0])
    reduce_end(0, started)
    started = reduce_start(1)
    corner_down = strip(bands[1])
    fold_band(corner_up, bands[0], send_up)
    vertical((0, 1), ())
    reduce_end(1, started)
    started = reduce_start(2)
    fold_band(corner_down, bands[1], send_down)
    vertical((2, 3), (0, 1))
    middle(0)
    reduce_end(2, started)
    steps = len(plan[0])
    started = reduce_start(3)
    vertical((4, 5), (2, 3))
    middle(1)
    reduce_end(3, started)
    for step in range(4, steps):
        started = reduce_start(step)
        reduce_end(step, started)

    for lane in range(lanes):
        s = state[lane]
        at = pl.ds(lane * lane_w, lane_w)
        keep = pl.ds(pl.multiple_of(s["off"], SUB), s["n"])
        weight = s["src"][planes - 1, keep, at] + 1e-05
        for k in range(2 * modes):
            out_probe[k, keep, at] = s["src"][k, keep, at] / weight

    def gather_start(level):
        started = []
        for lane in range(lanes):
            s = state[lane]
            size, mine, peers, split = history[lane][level]
            at = pl.ds(lane * lane_w, lane_w)
            if split:
                own = out_probe.at[:, pl.ds(pl.multiple_of(s["off"], SUB), s["n"]), at]
                started += [send(own, own, device) for _, device in peers]
                s["off"] = s["off"] - mine * s["n"]
                s["n"] *= size
        return started

    def gather_end(started):
        for copy in started:
            copy.wait_recv()

    started = gather_start(steps - 1)
    vertical((6, 7), (4, 5))
    middle(2)
    power = jnp.zeros((extent, extent), F32)
    for k in range(modes):
        for c in range(2):
            power += probe[k, c] * probe[k, c]
    scale = jnp.max(power, keepdims=True) + 1e-06
    for level in range(steps - 2, 0, -1):
        gather_end(started)
        started = gather_start(level)
        if level == 2:
            vertical((), (6, 7))
            middle(3)
    gather_end(started)
    started = gather_start(0)
    for copy in folded:
        copy.wait_recv()
    for c in range(2):
        step_sum = acc[c, pl.ds(m, rows), pl.ds(m, cols)]
        gap_r = [jnp.zeros((rows - 2 * m, cols), F32)] if rows > 2 * m else []
        gap_c = [jnp.zeros((rows, cols - 2 * m), F32)] if cols > 2 * m else []
        side = jnp.concatenate(
            [from_left[c, pl.ds(m, rows), :]] + gap_c + [from_right[c, pl.ds(m, rows), :]], 1
        )
        ends = jnp.concatenate([from_up[c]] + gap_r + [from_down[c]], 0)
        out_obj[c] = (step_sum + side + ends) / scale
    gather_end(started)
    for copy in pending:
        copy.wait_send()


def body(n_gx, n_gy, object_field, probe_field, amplitude, offsets):
    extent = probe_field.shape[-1]
    modes = probe_field.shape[0]
    margin = extent // 2
    rows, cols = object_field.shape[1:]
    positions = amplitude.shape[0]
    ext_shape = (2, rows + 2 * margin + SUB, cols + 2 * margin)
    ext = pl.pallas_call(
        functools.partial(halo_kernel, n_gx, n_gy, margin),
        out_shape=jax.ShapeDtypeStruct(ext_shape, F32),
        in_specs=[ANY],
        out_specs=VMEM,
        scratch_shapes=[pltpu.SemaphoreType.DMA((2, 2 + 6 * STRIPS)), pltpu.SemaphoreType.DMA((1,))],
        compiler_params=pltpu.CompilerParams(collective_id=0, has_side_effects=True, vmem_limit_bytes=LIMIT),
        name="halo",
    )(object_field)

    planes = 2 * modes + 1
    acc, sums = pl.pallas_call(
        functools.partial(update_kernel, margin),
        grid=(positions,),
        out_shape=(
            jax.ShapeDtypeStruct(ext_shape, F32),
            jax.ShapeDtypeStruct((planes, extent, extent), F32),
        ),
        in_specs=[
            pl.BlockSpec(memory_space=pltpu.SMEM),
            VMEM,
            VMEM,
            pl.BlockSpec((1, extent, extent), lambda i: (i, 0, 0)),
            VMEM,
        ],
        out_specs=(VMEM, VMEM),
        scratch_shapes=[
            pltpu.VMEM((2, extent, extent), F32),
            pltpu.VMEM((modes, 2, extent, extent), F32),
            pltpu.VMEM((2 * extent, modes * extent), BF16),
            pltpu.VMEM((modes * extent, 2 * extent), BF16),
            pltpu.VMEM((modes * extent, 2 * extent), F32),
            pltpu.VMEM((2 * extent, 2 * extent), BF16),
            pltpu.VMEM((2 * extent, 2 * extent), BF16),
        ],
        compiler_params=pltpu.CompilerParams(vmem_limit_bytes=LIMIT),
        name="update",
    )(offsets.transpose(1, 2, 0), ext, probe_field, amplitude[:, 0], dft_tables(extent))

    plan = reduce_plan(n_gx, n_gy)[0]
    steps = len(plan)
    peers = sum((1 << count) - 1 for _, _, count in plan)
    out_obj, out_probe = pl.pallas_call(
        functools.partial(fold_kernel, n_gx, n_gy, margin),
        out_shape=(
            jax.ShapeDtypeStruct(object_field.shape, F32),
            jax.ShapeDtypeStruct((2 * modes, extent, extent), F32),
        ),
        in_specs=[VMEM] * 4,
        out_specs=(VMEM, VMEM),
        scratch_shapes=[
            pltpu.VMEM((2, rows + 2 * margin, margin), F32),
            pltpu.VMEM((2, rows + 2 * margin, margin), F32),
            pltpu.VMEM((2, margin, cols), F32),
            pltpu.VMEM((2, margin, cols), F32),
            pltpu.VMEM((2, margin, cols), F32),
            pltpu.VMEM((2, margin, cols), F32),
            pltpu.VMEM((steps, planes, extent, extent), F32),
            pltpu.VMEM((planes, 3 * extent, extent), F32),
            pltpu.SemaphoreType.DMA((2, 4 + 2 * PIECES + 2 * MIDS + 4 * peers)),
        ],
        compiler_params=pltpu.CompilerParams(collective_id=1, has_side_effects=True, vmem_limit_bytes=LIMIT),
        name="fold",
    )(acc, object_field, probe_field, sums)
    return object_field + out_obj, probe_field + out_probe.reshape(probe_field.shape)


def solution(mesh):
    in_specs = (P(None, "gx", "gy"), P(), P("gx", "gy", None, None), P("gx", "gy", None))
    out_specs = (P(None, "gx", "gy"), P())
    step = functools.partial(body, mesh.shape["gx"], mesh.shape["gy"])
    return jax.shard_map(step, mesh=mesh, in_specs=in_specs, out_specs=out_specs, check_vma=False)
```

```python
import functools
import math

import jax
import jax.numpy as jnp
import numpy as np
from jax import lax
from jax.experimental import pallas as pl
from jax.experimental.pallas import tpu as pltpu
from jax.sharding import PartitionSpec as P

MESH = pl.DeviceIdType.MESH
VMEM = pl.BlockSpec(memory_space=pltpu.VMEM)
HBM = pl.BlockSpec(memory_space=pltpu.MemorySpace.HBM)
F32 = jnp.float32
BF16 = jnp.bfloat16
CHUNK = 32
SUB = 8
STRIPS = 2
PIECES = 2
MIDS = 2
LIMIT = 30 << 20


def dft_tables(extent):
    indices = np.arange(extent)
    angles = (indices[:, None] * indices[None, :] % extent) * (2.0 * math.pi / extent)
    norm_factor = 1.0 / math.sqrt(extent)
    both = np.concatenate([np.cos(angles), np.sin(angles)], 1) * norm_factor
    return jnp.asarray(both.astype(np.float32).astype(jnp.bfloat16))


def remote(src, dst, sems, slot, device):
    return pltpu.make_async_remote_copy(
        src_ref=src,
        dst_ref=dst,
        send_sem=sems.at[0, slot],
        recv_sem=sems.at[1, slot],
        device_id=device,
        device_id_type=MESH,
    )


def greet(devices):
    barrier = pltpu.get_barrier_semaphore()
    for device in devices:
        pl.semaphore_signal(barrier, inc=1, device_id=device, device_id_type=MESH)
    pl.semaphore_wait(barrier, len(devices))


def halo_kernel(n_gx, n_gy, margin, obj, ext, sems, local_sem):
    gx, gy = lax.axis_index("gx"), lax.axis_index("gy")
    rows, cols = obj.shape[1], obj.shape[2]
    m = margin
    odd = lax.rem(gy, 2)
    up = (lax.rem(gx + n_gx - 1, n_gx), gy)
    down = (lax.rem(gx + 1, n_gx), gy)
    step_y = 1 - 2 * odd
    near = (gx, gy + step_y)
    far = (gx, lax.rem(gy - step_y + n_gy, n_gy))
    sides = (near, far)
    half_at = (pl.multiple_of((1 - odd) * (cols - m), m), pl.multiple_of(odd * (cols - m), m))
    lands_at = (pl.multiple_of(odd * (m + cols), m), pl.multiple_of((1 - odd) * (m + cols), m))
    own = pltpu.make_async_copy(obj, ext.at[:, pl.ds(m, rows), pl.ds(m, cols)], local_sem.at[0])
    own.start()
    greet((up, down, near, far))
    slot = [0]
    pending = []

    def send(src, dst, device):
        copy = remote(src, dst, sems, slot[0], device)
        slot[0] += 1
        copy.start()
        pending.append(copy)
        return copy

    piece = m // STRIPS
    ways = ((0, m + rows, up), (rows - m, 0, down))
    arrivals = []
    waits = []

    def middle(side):
        src = obj.at[:, :, pl.ds(half_at[side], m)]
        dst = ext.at[:, pl.ds(m, rows), pl.ds(lands_at[side], m)]
        waits.append(send(src, dst, sides[side]))

    def vertical(side):
        for i in range(STRIPS):
            for src_row, dst_row, device in ways:
                band = pl.ds(dst_row + i * piece, piece)
                src = obj.at[:, pl.ds(src_row + i * piece, piece), pl.ds(half_at[side], m)]
                dst = ext.at[:, band, pl.ds(m + half_at[side], m)]
                arrivals.append((send(src, dst, device), side, band))

    vertical(1)
    middle(1)
    vertical(0)
    middle(0)
    for copy, side, band in arrivals:
        copy.wait_recv()
        src = ext.at[:, band, pl.ds(m + half_at[side], m)]
        waits.append(send(src, ext.at[:, band, pl.ds(lands_at[side], m)], sides[side]))
    for copy in waits:
        copy.wait_recv()
    for copy in pending:
        copy.wait_send()
    own.wait()


def update_kernel(
    margin, offs, ext, probe, amp, table, acc, sums, win, psi, xbuf, ybuf, far, fr, frt
):
    p = pl.program_id(0)
    extent = probe.shape[-1]
    modes = probe.shape[0]
    width = ext.shape[2]
    r0 = offs[0, 0, p] + margin
    c0 = offs[0, 1, p] + margin
    back_shift = lax.rem(width - c0, width)
    low = lax.rem(r0, SUB)
    base = r0 - low
    tall = CHUNK + SUB
    row_shift = lax.rem(tall - low, tall)
    n_chunks = extent // CHUNK

    @pl.when(p == 0)
    def _():
        acc[...] = jnp.zeros_like(acc)
        sums[...] = jnp.zeros_like(sums)
        c, s = table[:, :extent], table[:, extent:]
        fr[:extent, :extent] = c
        fr[:extent, extent:] = s
        fr[extent:, :extent] = -s
        fr[extent:, extent:] = c
        frt[:extent, :extent] = c
        frt[:extent, extent:] = -s
        frt[extent:, :extent] = s
        frt[extent:, extent:] = c

    @pl.loop(0, n_chunks, unroll=8)
    def _(i):
        rb = pl.multiple_of(i * CHUNK, CHUNK)
        here = pl.ds(rb, CHUNK)
        w = []
        for part in range(2):
            line = ext[part, pl.ds(pl.multiple_of(base + rb, SUB), tall), :]
            line = pltpu.roll(line, row_shift, 0)[:CHUNK]
            w.append(pltpu.roll(line, back_shift, 1)[:, :extent])
            win[part, here, :] = w[part]
        sums[0, here, :] += w[0] * w[0] + w[1] * w[1]
        for k in range(modes):
            cols = slice(k * extent, (k + 1) * extent)
            pr, pi = probe[k, 0, here, :], probe[k, 1, here, :]
            psi_re = pr * w[0] - pi * w[1]
            psi_im = pr * w[1] + pi * w[0]
            psi[k, 0, here, :] = psi_re
            psi[k, 1, here, :] = psi_im
            xbuf[here, cols] = psi_re.astype(BF16)
            xbuf[pl.ds(extent + rb, CHUNK), cols] = psi_im.astype(BF16)

    def rows_then_cols(row_table, col_table):
        for part in range(2):
            table = row_table[part * extent : (part + 1) * extent, :]
            out = jnp.dot(table, xbuf[...], preferred_element_type=F32).astype(BF16)
            for k in range(modes):
                ybuf[k * extent : (k + 1) * extent, part * extent : (part + 1) * extent] = out[
                    :, k * extent : (k + 1) * extent
                ]
        for k in range(modes):
            band = slice(k * extent, (k + 1) * extent)
            far[band, :] = jnp.dot(ybuf[band, :], col_table[...], preferred_element_type=F32)

    rows_then_cols(fr, frt)

    @pl.loop(0, n_chunks, unroll=8)
    def _(i):
        rb = pl.multiple_of(i * CHUNK, CHUNK)
        parts = []
        intensity = jnp.zeros((CHUNK, extent), F32)
        for k in range(modes):
            at = pl.ds(k * extent + rb, CHUNK)
            re, im = far[at, :extent], far[at, extent:]
            intensity += re * re + im * im
            parts.append((re, im))
        factor = amp[0, pl.ds(rb, CHUNK), :] * jnp.minimum(lax.rsqrt(intensity), 4.0)
        for k in range(modes):
            cols = slice(k * extent, (k + 1) * extent)
            xbuf[pl.ds(rb, CHUNK), cols] = (parts[k][0] * factor).astype(BF16)
            xbuf[pl.ds(extent + rb, CHUNK), cols] = (parts[k][1] * factor).astype(BF16)

    rows_then_cols(frt, fr)

    @pl.loop(0, n_chunks, unroll=8)
    def _(i):
        rb = pl.multiple_of(i * CHUNK, CHUNK)
        here = pl.ds(rb, CHUNK)
        wr, wi = win[0, here, :], win[1, here, :]
        obj_re = jnp.zeros((CHUNK, extent), F32)
        obj_im = jnp.zeros((CHUNK, extent), F32)
        for k in range(modes):
            at = pl.ds(k * extent + rb, CHUNK)
            dr = far[at, :extent] - psi[k, 0, here, :]
            di = far[at, extent:] - psi[k, 1, here, :]
            pr, pi = probe[k, 0, here, :], probe[k, 1, here, :]
            obj_re += pr * dr + pi * di
            obj_im += pr * di - pi * dr
            sums[2 * k + 1, here, :] += wr * dr + wi * di
            sums[2 * k + 2, here, :] += wr * di - wi * dr
        blank = jnp.zeros((CHUNK, width - extent), F32)
        below = jnp.zeros((SUB, width), F32)
        for part, value in enumerate((obj_re, obj_im)):
            line = pltpu.roll(jnp.concatenate([value, blank], 1), lax.rem(c0, width), 1)
            line = pltpu.roll(jnp.concatenate([line, below], 0), low, 0)
            acc[part, pl.ds(pl.multiple_of(base + rb, SUB), tall), :] += line


def reduce_plan(n_gx, n_gy):
    x_bits, y_bits = n_gx.bit_length() - 1, n_gy.bit_length() - 1
    steps = [(0, 0, 0, 1), (0, 1, 1, 1)]
    steps.append((1, min(2, x_bits - 1), 0, 0))
    for b in range(3, x_bits, 2):
        steps.append((b, min(2, x_bits - b), 0, 0))
    for b in range(2, y_bits, 2):
        steps.append((0, 0, b, min(2, y_bits - b)))
    return steps


def fold_schedule(steps, n):
    bands = [(b, i) for i in range(PIECES) for b in (0, 1)]
    near_bands = [("vert", 0, b, i) for b, i in bands]
    far_bands = [("vert", 1, b, i) for b, i in bands]
    half = len(far_bands) // 2
    acts = [("rs", 0, c) for c in range(n)]
    acts += [("corner", 0, b, i) for b, i in bands] + [("power",)]
    for c in range(n):
        acts += [("rse", 0, c), ("rs", 1, c)]
    acts += [("corner", 1, b, i) for b, i in bands] + near_bands
    for c in range(n):
        acts += [("rse", 1, c), ("rs", 2, c)]
    acts += [("mid", side, i, MIDS) for side in (1, 0) for i in range(MIDS)] + far_bands[:half]
    for s in range(2, steps):
        for c in range(n):
            acts.append(("rse", s, c))
            acts += [("rs", s + 1, c)] if s + 1 < steps else [("div", c), ("agz", c)]
    acts += far_bands[half:]
    for name in ("agp", "agc", "age"):
        acts += [(name, c) for c in range(n)]
    return acts + [("finish",)]


def fold_kernel(n_gx, n_gy, margin, chunks, acc, probe, sums, out_obj, out_probe, *scratch):
    (from_near, from_far, vsend, vrecv, part, inbox, sems) = scratch
    gx, gy = lax.axis_index("gx"), lax.axis_index("gy")
    rows, cols = out_obj.shape[1], out_obj.shape[2]
    planes, extent = sums.shape[0], sums.shape[1]
    modes = probe.shape[0]
    m = margin
    odd = lax.rem(gy, 2)
    up = (lax.rem(gx + n_gx - 1, n_gx), gy)
    down = (lax.rem(gx + 1, n_gx), gy)
    step_y = 1 - 2 * odd
    near = (gx, gy + step_y)
    far = (gx, lax.rem(gy - step_y + n_gy, n_gy))
    sides = (near, far)
    came = (from_near, from_far)
    halo_at = (pl.multiple_of((1 - odd) * (m + cols), m), pl.multiple_of(odd * (m + cols), m))
    half_at = (pl.multiple_of(m + (1 - odd) * (cols - m), m), pl.multiple_of(m + odd * (cols - m), m))
    plan = reduce_plan(n_gx, n_gy)
    steps = len(plan)

    def swap(field, d, bits):
        out = 0
        for b in range(bits):
            bit = lax.rem(field // (1 << b), 2)
            out = out + (1 << b) * (1 - bit if d >> b & 1 else bit)
        return out

    def members(bx, cx, by, cy):
        nx, ny = 1 << cx, 1 << cy
        fx, fy = lax.rem(gx // (1 << bx), nx), lax.rem(gy // (1 << by), ny)
        peers = []
        for dy in range(ny):
            for dx in range(nx):
                if dx or dy:
                    px, py = swap(fx, dx, cx), swap(fy, dy, cy)
                    peers.append((px + nx * py, (gx + (px - fx) * (1 << bx), gy + (py - fy) * (1 << by))))
        return nx * ny, fx + nx * fy, peers

    greet([up, down, near, far] + [dev for g in plan for _, dev in members(*g)[2]])

    slot = [0]
    pending = []

    def send(src, dst, device):
        copy = remote(src, dst, sems, slot[0], device)
        slot[0] += 1
        copy.start()
        pending.append(copy)
        return copy

    state = [{"off": 0, "n": extent, "src": sums, "box": 0} for _ in chunks]
    history = [[] for _ in chunks]
    flight = {}

    def rws(at, n):
        return pl.ds(pl.multiple_of(at, SUB), n)

    def rs(step, c):
        lo, hi = chunks[c]
        s = state[c]
        size, mine, peers = members(*plan[step])
        split = step < 3
        n = s["n"] // size if split else s["n"]
        copies = []
        for field, device in peers:
            give = s["off"] + field * n if split else s["off"]
            box = s["box"] + mine * n
            copies.append(send(s["src"].at[lo:hi, rws(give, n), :], inbox.at[lo:hi, rws(box, n), :], device))
        keep = s["off"] + mine * n if split else s["off"]
        history[c].append((size, mine, peers, split))
        flight["rs", step, c] = (copies, keep, n, size, mine, [f for f, _ in peers], s["box"], split)
        s["box"] += size * n

    def rse(step, c):
        lo, hi = chunks[c]
        copies, keep, n, size, mine, fields, box, split = flight.pop(("rs", step, c))
        s = state[c]
        for copy in copies:
            copy.wait_recv()
        own = s["src"][lo:hi, rws(keep, n), :]
        if split:
            total = own
            for f in fields:
                total += inbox[lo:hi, rws(box + f * n, n), :]
        else:
            inbox[lo:hi, rws(box + mine * n, n), :] = own
            total = inbox[lo:hi, rws(box, n), :]
            for j in range(1, size):
                total += inbox[lo:hi, rws(box + j * n, n), :]
        part[step, lo:hi, rws(keep, n), :] = total
        s["off"], s["n"], s["src"] = keep, n, part.at[step]

    def div(c):
        lo, hi = chunks[c]
        first = 1 if lo == 0 else 0
        s = state[c]
        keep = rws(s["off"], s["n"])
        weight = s["src"][0, keep, :] + 1e-05
        for k in range(lo + first, hi):
            out_probe[k - 1, keep, :] = s["src"][k, keep, :] / weight

    def planes_of(c):
        lo, hi = chunks[c][:2]
        return max(lo - 1, 0), hi - 1

    def give(c, off, n, device):
        lo, hi = planes_of(c)
        own = out_probe.at[lo:hi, rws(off, n), :]
        return send(own, own, device)

    def agz(c):
        off, n = state[c]["off"], state[c]["n"]
        _, _, z_peers, _ = history[c][2]
        _, _, p_peers, _ = history[c][1]
        zs = [give(c, off, n, device) for _, device in z_peers]
        ps = [[give(c, off, n, device)] for _, device in p_peers]
        flight["agz", c] = (zs, ps)

    def agp(c):
        off, n = state[c]["off"], state[c]["n"]
        z_size, z_mine, z_peers, _ = history[c][2]
        _, _, p_peers, _ = history[c][1]
        _, _, ((_, partner),), _ = history[c][0]
        zs, ps = flight.pop(("agz", c))
        base = off - z_mine * n
        for (field, _), copy in zip(z_peers, zs):
            copy.wait_recv()
            for (_, device), got in zip(p_peers, ps):
                got.append(give(c, base + field * n, n, device))
        flight["agp", c] = (ps, base, n * z_size, [give(c, base, n * z_size, partner)])

    def agc(c):
        ps, base, n, cs = flight.pop(("agp", c))
        p_size, p_mine, p_peers, _ = history[c][1]
        _, _, ((_, partner),), _ = history[c][0]
        for (field, _), copies in zip(p_peers, ps):
            for copy in copies:
                copy.wait_recv()
            cs.append(give(c, base + (field - p_mine) * n, n, partner))
        flight["agc", c] = cs

    def age(c):
        for copy in flight.pop(("agc", c)):
            copy.wait_recv()

    band_at = (0, m + rows)
    piece = m // PIECES

    def corner(side, b, i):
        band = pl.ds(band_at[b] + i * piece, piece)
        flight["corner", side, b, i] = send(acc.at[:, band, pl.ds(halo_at[side], m)], came[side].at[:, band, :], sides[side])

    def mid(side, i, of):
        band = pl.ds(m + i * (rows // of), rows // of)
        flight["mid", side, i] = send(acc.at[:, band, pl.ds(halo_at[side], m)], came[side].at[:, band, :], sides[side])

    def vert(side, b, i):
        flight.pop(("corner", side, b, i)).wait_recv()
        band = pl.ds(band_at[b] + i * piece, piece)
        here = pl.ds(i * piece, piece)
        vsend[b, side, :, here, :] = acc[:, band, pl.ds(half_at[side], m)] + came[side][:, band, :]
        flight["vert", side, b, i] = send(vsend.at[b, side, :, here, :], vrecv.at[b, side, :, here, :], (up, down)[b])

    power_box = []
    def power():
        total = jnp.zeros((extent, extent), F32)
        for k in range(modes):
            for c in range(2):
                total += probe[k, c] * probe[k, c]
        power_box.append(jnp.max(total, keepdims=True) + 1e-06)

    def finish():
        scale = power_box[0]
        for key in [k for k in flight if k[0] in ("mid", "vert")]:
            flight.pop(key).wait_recv()
        for side in range(2):
            own = pl.ds(half_at[side], m)
            dst = pl.ds(pl.multiple_of(half_at[side] - m, m), m)
            for c in range(2):
                base = acc[c, pl.ds(m, rows), own] + came[side][c, pl.ds(m, rows), :]
                ends = jnp.concatenate([vrecv[1, side, c], vrecv[0, side, c]], 0)
                out_obj[c, :, dst] = (base + ends) / scale

    ops = {"rs": rs, "rse": rse, "div": div, "agz": agz, "agp": agp, "agc": agc, "age": age, "corner": corner, "mid": mid, "vert": vert, "power": power, "finish": finish}
    for name, *args in fold_schedule(steps, len(chunks)):
        ops[name](*args)
    assert not flight, flight
    for copy in pending:
        copy.wait_send()


def body(n_gx, n_gy, object_field, probe_field, amplitude, offsets):
    extent = probe_field.shape[-1]
    modes = probe_field.shape[0]
    margin = extent // 2
    rows, cols = object_field.shape[1:]
    positions = amplitude.shape[0]
    ext_shape = (2, rows + 2 * margin + SUB, cols + 2 * margin)
    ext = pl.pallas_call(
        functools.partial(halo_kernel, n_gx, n_gy, margin),
        out_shape=jax.ShapeDtypeStruct(ext_shape, F32),
        in_specs=[HBM],
        out_specs=VMEM,
        scratch_shapes=[pltpu.SemaphoreType.DMA((2, 2 + 8 * STRIPS)), pltpu.SemaphoreType.DMA((1,))],
        compiler_params=pltpu.CompilerParams(collective_id=0, has_side_effects=True, vmem_limit_bytes=LIMIT),
        name="halo",
    )(object_field)

    planes = 2 * modes + 1
    acc, sums = pl.pallas_call(
        functools.partial(update_kernel, margin),
        grid=(positions,),
        out_shape=(
            jax.ShapeDtypeStruct(ext_shape, F32),
            jax.ShapeDtypeStruct((planes, extent, extent), F32),
        ),
        in_specs=[
            pl.BlockSpec(memory_space=pltpu.SMEM),
            VMEM,
            VMEM,
            pl.BlockSpec((1, extent, extent), lambda i: (i, 0, 0)),
            VMEM,
        ],
        out_specs=(VMEM, VMEM),
        scratch_shapes=[
            pltpu.VMEM((2, extent, extent), F32),
            pltpu.VMEM((modes, 2, extent, extent), F32),
            pltpu.VMEM((2 * extent, modes * extent), BF16),
            pltpu.VMEM((modes * extent, 2 * extent), BF16),
            pltpu.VMEM((modes * extent, 2 * extent), F32),
            pltpu.VMEM((2 * extent, 2 * extent), BF16),
            pltpu.VMEM((2 * extent, 2 * extent), BF16),
        ],
        compiler_params=pltpu.CompilerParams(vmem_limit_bytes=LIMIT),
        name="update",
    )(offsets.transpose(1, 2, 0), ext, probe_field, amplitude[:, 0], dft_tables(extent))

    plan = reduce_plan(n_gx, n_gy)
    peers = sum((1 << (cx + cy)) - 1 for _, cx, _, cy in plan)
    chunks = ((0, modes + 1), (modes + 1, planes))
    out_obj, out_probe = pl.pallas_call(
        functools.partial(fold_kernel, n_gx, n_gy, margin, chunks),
        out_shape=(
            jax.ShapeDtypeStruct(object_field.shape, F32),
            jax.ShapeDtypeStruct((2 * modes, extent, extent), F32),
        ),
        in_specs=[VMEM] * 3,
        out_specs=(VMEM, VMEM),
        scratch_shapes=[
            pltpu.VMEM((2, rows + 2 * margin, margin), F32),
            pltpu.VMEM((2, rows + 2 * margin, margin), F32),
            pltpu.VMEM((2, 2, 2, margin, margin), F32),
            pltpu.VMEM((2, 2, 2, margin, margin), F32),
            pltpu.VMEM((len(plan), planes, extent, extent), F32),
            pltpu.VMEM((planes, 3 * extent, extent), F32),
            pltpu.SemaphoreType.DMA((2, 8 * PIECES + 2 * MIDS + (peers + 24) * len(chunks))),
        ],
        compiler_params=pltpu.CompilerParams(
            collective_id=1, has_side_effects=True, vmem_limit_bytes=LIMIT
        ),
        name="fold",
    )(acc, probe_field, sums)
    return object_field + out_obj, probe_field + out_probe.reshape(probe_field.shape)


def solution(mesh):
    in_specs = (P(None, "gx", "gy"), P(), P("gx", "gy", None, None), P("gx", "gy", None))
    out_specs = (P(None, "gx", "gy"), P())
    step = functools.partial(body, mesh.shape["gx"], mesh.shape["gy"])
    return jax.shard_map(step, mesh=mesh, in_specs=in_specs, out_specs=out_specs, check_vma=False)
```

```python
import functools
import math

import jax
import jax.numpy as jnp
import numpy as np
from jax import lax
from jax.experimental import pallas as pl
from jax.experimental.pallas import tpu as pltpu
from jax.sharding import PartitionSpec as P

MESH = pl.DeviceIdType.MESH
VMEM = pl.BlockSpec(memory_space=pltpu.VMEM)
HBM = pl.BlockSpec(memory_space=pltpu.MemorySpace.HBM)
F32 = jnp.float32
BF16 = jnp.bfloat16
CHUNK = 32
SUB = 8
LANE = 128
STRIPS = 2
PIECES = 2
MIDS = 2
LIMIT = 30 << 20


def dft_tables(extent):
    indices = np.arange(extent)
    angles = (indices[:, None] * indices[None, :] % extent) * (2.0 * math.pi / extent)
    norm_factor = 1.0 / math.sqrt(extent)
    both = np.concatenate([np.cos(angles), np.sin(angles)], 1) * norm_factor
    return jnp.asarray(both.astype(np.float32).astype(jnp.bfloat16))


def remote(src, dst, sems, slot, device):
    return pltpu.make_async_remote_copy(
        src_ref=src,
        dst_ref=dst,
        send_sem=sems.at[0, slot],
        recv_sem=sems.at[1, slot],
        device_id=device,
        device_id_type=MESH,
    )


def greet(devices):
    barrier = pltpu.get_barrier_semaphore()
    for device in devices:
        pl.semaphore_signal(barrier, inc=1, device_id=device, device_id_type=MESH)
    pl.semaphore_wait(barrier, len(devices))


def halo_kernel(n_gx, n_gy, margin, obj, ext, sems, local_sem):
    gx, gy = lax.axis_index("gx"), lax.axis_index("gy")
    rows, cols = obj.shape[1], obj.shape[2]
    m = margin
    mt, ct = m // LANE, cols // LANE
    odd = lax.rem(gy, 2)
    up = (lax.rem(gx + n_gx - 1, n_gx), gy)
    down = (lax.rem(gx + 1, n_gx), gy)
    step_y = 1 - 2 * odd
    near = (gx, gy + step_y)
    far = (gx, lax.rem(gy - step_y + n_gy, n_gy))
    sides = (near, far)
    half_at = ((1 - odd) * (ct - mt), odd * (ct - mt))
    lands_at = (odd * (mt + ct), (1 - odd) * (mt + ct))
    owns = [
        pltpu.make_async_copy(
            obj.at[:, :, pl.ds(t * LANE, LANE)], ext.at[:, mt + t, pl.ds(m, rows), :], local_sem.at[t]
        )
        for t in range(ct)
    ]
    for own in owns:
        own.start()
    greet((up, down, near, far))
    slot = [0]
    pending = []

    def send(src, dst, device):
        copy = remote(src, dst, sems, slot[0], device)
        slot[0] += 1
        copy.start()
        pending.append(copy)
        return copy

    piece = m // STRIPS
    ways = ((0, m + rows, up), (rows - m, 0, down))
    arrivals = []
    waits = []

    def lanes(side, t):
        return pl.ds(pl.multiple_of((half_at[side] + t) * LANE, LANE), LANE)

    def middle(side):
        for t in range(mt):
            dst = ext.at[:, lands_at[side] + t, pl.ds(m, rows), :]
            waits.append(send(obj.at[:, :, lanes(side, t)], dst, sides[side]))

    def vertical(side):
        for i in range(STRIPS):
            for src_row, dst_row, device in ways:
                band = pl.ds(dst_row + i * piece, piece)
                for t in range(mt):
                    src = obj.at[:, pl.ds(src_row + i * piece, piece), lanes(side, t)]
                    dst = ext.at[:, mt + half_at[side] + t, band, :]
                    arrivals.append((send(src, dst, device), side, band, t))

    vertical(1)
    middle(1)
    vertical(0)
    middle(0)
    for copy, side, band, t in arrivals:
        copy.wait_recv()
        src = ext.at[:, mt + half_at[side] + t, band, :]
        waits.append(send(src, ext.at[:, lands_at[side] + t, band, :], sides[side]))
    for copy in waits:
        copy.wait_recv()
    for copy in pending:
        copy.wait_send()
    for own in owns:
        own.wait()


def update_kernel(margin, offs, ext, probe, amp, table, acc, sums, win, psi, xbuf, ybuf, far, fr, frt):
    positions = amp.shape[0]
    extent = probe.shape[-1]
    modes = probe.shape[0]
    last = ext.shape[1] - extent // LANE - 1
    starts = range(0, extent, CHUNK)

    c, s = table[:, :extent], table[:, extent:]
    fr[:extent, :extent] = c
    fr[:extent, extent:] = s
    fr[extent:, :extent] = -s
    fr[extent:, extent:] = c
    frt[:extent, :extent] = c
    frt[:extent, extent:] = -s
    frt[extent:, :extent] = s
    frt[extent:, extent:] = c

    lane = lax.broadcasted_iota(jnp.int32, (CHUNK, LANE), 1)

    def place(p):
        c0 = offs[0, 1, p] + margin
        tile = jnp.minimum(c0 // LANE, last)
        return offs[0, 0, p] + margin, tile, c0 - tile * LANE

    def add(plane, here, value, p):
        if p == 0:
            sums[plane, here, :] = value
        else:
            sums[plane, here, :] += value

    def extract(p, rb):
        r0, tile, low = place(p)
        here = pl.ds(rb, CHUNK)
        q = p % 2
        w = []
        for part in range(2):
            line = [
                pltpu.roll(ext[part, tile + t, pl.ds(r0 + rb, CHUNK), :], lax.rem(LANE - low, LANE), 1)
                for t in range(extent // LANE + 1)
            ]
            line = [jnp.where(lane < LANE - low, a, b) for a, b in zip(line, line[1:])]
            w.append(jnp.concatenate(line, 1))
            win[q, part, here, :] = w[part]
        add(0, here, w[0] * w[0] + w[1] * w[1], p)
        for k in range(modes):
            cols = slice(k * extent, (k + 1) * extent)
            pr, pi = probe[k, 0, here, :], probe[k, 1, here, :]
            psi_re = pr * w[0] - pi * w[1]
            psi_im = pr * w[1] + pi * w[0]
            psi[q, k, 0, here, :] = psi_re
            psi[q, k, 1, here, :] = psi_im
            xbuf[q, here, cols] = psi_re.astype(BF16)
            xbuf[q, pl.ds(extent + rb, CHUNK), cols] = psi_im.astype(BF16)

    def rows_pass(q, row_table, part):
        band = row_table[part * extent : (part + 1) * extent, :]
        out = jnp.dot(band, xbuf[q], preferred_element_type=F32).astype(BF16)
        for k in range(modes):
            ybuf[k * extent : (k + 1) * extent, part * extent : (part + 1) * extent] = out[
                :, k * extent : (k + 1) * extent
            ]

    def cols_pass(q, col_table, k):
        band = slice(k * extent, (k + 1) * extent)
        far[q, band, :] = jnp.dot(ybuf[band, :], col_table[...], preferred_element_type=F32)

    def project(p, rb):
        q = p % 2
        parts = []
        intensity = jnp.zeros((CHUNK, extent), F32)
        for k in range(modes):
            at = pl.ds(k * extent + rb, CHUNK)
            re, im = far[q, at, :extent], far[q, at, extent:]
            intensity += re * re + im * im
            parts.append((re, im))
        factor = amp[p, pl.ds(rb, CHUNK), :] * jnp.minimum(lax.rsqrt(intensity), 4.0)
        for k in range(modes):
            cols = slice(k * extent, (k + 1) * extent)
            xbuf[q, pl.ds(rb, CHUNK), cols] = (parts[k][0] * factor).astype(BF16)
            xbuf[q, pl.ds(extent + rb, CHUNK), cols] = (parts[k][1] * factor).astype(BF16)

    def correct(p, rb):
        r0, tile, low = place(p)
        q = p % 2
        here = pl.ds(rb, CHUNK)
        wr, wi = win[q, 0, here, :], win[q, 1, here, :]
        obj_re = jnp.zeros((CHUNK, extent), F32)
        obj_im = jnp.zeros((CHUNK, extent), F32)
        for k in range(modes):
            at = pl.ds(k * extent + rb, CHUNK)
            dr = far[q, at, :extent] - psi[q, k, 0, here, :]
            di = far[q, at, extent:] - psi[q, k, 1, here, :]
            pr, pi = probe[k, 0, here, :], probe[k, 1, here, :]
            obj_re += pr * dr + pi * di
            obj_im += pr * di - pi * dr
            add(2 * k + 1, here, wr * dr + wi * di, p)
            add(2 * k + 2, here, wr * di - wi * dr, p)
        blank = jnp.zeros((CHUNK, LANE), F32)
        for part, value in enumerate((obj_re, obj_im)):
            line = [
                pltpu.roll(value[:, t * LANE : (t + 1) * LANE], lax.rem(low, LANE), 1)
                for t in range(extent // LANE)
            ]
            for t, (a, b) in enumerate(zip([blank] + line, line + [blank])):
                acc[part, tile + t, pl.ds(r0 + rb, CHUNK), :] += jnp.where(lane < low, a, b)

    def clear(part, t):
        acc[part, t] = jnp.zeros(acc.shape[2:], F32)

    def beside(matmuls, others):
        n = len(matmuls)
        for i, (call, args) in enumerate(matmuls):
            call(*args)
            for other, rest in others[i * len(others) // n : (i + 1) * len(others) // n]:
                other(*rest)

    for rb in starts:
        extract(0, rb)
    for p in range(positions):
        q = p % 2
        there = [(rows_pass, (q, fr, 0)), (rows_pass, (q, fr, 1))]
        there += [(cols_pass, (q, frt, k)) for k in range(modes)]
        back = [(rows_pass, (q, frt, 0)), (rows_pass, (q, frt, 1))]
        back += [(cols_pass, (q, fr, k)) for k in range(modes)]
        beside(there, [(correct, (p - 1, rb)) for rb in starts] if p else [(clear, (i, t)) for i in range(2) for t in range(acc.shape[1])])
        for rb in starts:
            project(p, rb)
        beside(back, [(extract, (p + 1, rb)) for rb in starts] if p + 1 < positions else [])
    for rb in starts:
        correct(positions - 1, rb)


def reduce_plan(n_gx, n_gy):
    x_bits, y_bits = n_gx.bit_length() - 1, n_gy.bit_length() - 1
    steps = [(0, 0, 0, 1), (0, 1, 1, 1)]
    steps.append((1, min(2, x_bits - 1), 0, 0))
    for b in range(3, x_bits, 2):
        steps.append((b, min(2, x_bits - b), 0, 0))
    for b in range(2, y_bits, 2):
        steps.append((0, 0, b, min(2, y_bits - b)))
    return steps


def fold_schedule(steps, n):
    bands = [(b, i) for i in range(PIECES) for b in (0, 1)]
    near_bands = [("vert", 0, b, i) for b, i in bands]
    far_bands = [("vert", 1, b, i) for b, i in bands]
    half = len(far_bands) // 2
    acts = [("rs", 0, c) for c in range(n)]
    acts += [("corner", 0, b, i) for b, i in bands] + [("power",)]
    for c in range(n):
        acts += [("rse", 0, c), ("rs", 1, c)]
    acts += [("corner", 1, b, i) for b, i in bands] + near_bands
    for c in range(n):
        acts += [("rse", 1, c), ("rs", 2, c)]
    acts += [("mid", side, i, MIDS) for side in (1, 0) for i in range(MIDS)] + far_bands[:half]
    for s in range(2, steps):
        for c in range(n):
            acts.append(("rse", s, c))
            acts += [("rs", s + 1, c)] if s + 1 < steps else [("div", c), ("agz", c)]
    acts += far_bands[half:]
    for name in ("agp", "agc", "age"):
        acts += [(name, c) for c in range(n)]
    return acts + [("finish",)]


def fold_kernel(n_gx, n_gy, margin, chunks, acc, probe, sums, out_obj, out_probe, *scratch):
    (from_near, from_far, vsend, vrecv, part, inbox, sems) = scratch
    gx, gy = lax.axis_index("gx"), lax.axis_index("gy")
    rows, cols = out_obj.shape[1], out_obj.shape[2]
    planes, extent = sums.shape[0], sums.shape[1]
    modes = probe.shape[0]
    m = margin
    mt, ct = m // LANE, cols // LANE
    odd = lax.rem(gy, 2)
    up = (lax.rem(gx + n_gx - 1, n_gx), gy)
    down = (lax.rem(gx + 1, n_gx), gy)
    step_y = 1 - 2 * odd
    near = (gx, gy + step_y)
    far = (gx, lax.rem(gy - step_y + n_gy, n_gy))
    sides = (near, far)
    came = (from_near, from_far)
    halo_at = ((1 - odd) * (mt + ct), odd * (mt + ct))
    half_at = (mt + (1 - odd) * (ct - mt), mt + odd * (ct - mt))
    plan = reduce_plan(n_gx, n_gy)
    steps = len(plan)

    def swap(field, d, bits):
        out = 0
        for b in range(bits):
            bit = lax.rem(field // (1 << b), 2)
            out = out + (1 << b) * (1 - bit if d >> b & 1 else bit)
        return out

    def members(bx, cx, by, cy):
        nx, ny = 1 << cx, 1 << cy
        fx, fy = lax.rem(gx // (1 << bx), nx), lax.rem(gy // (1 << by), ny)
        peers = []
        for dy in range(ny):
            for dx in range(nx):
                if dx or dy:
                    px, py = swap(fx, dx, cx), swap(fy, dy, cy)
                    peers.append((px + nx * py, (gx + (px - fx) * (1 << bx), gy + (py - fy) * (1 << by))))
        return nx * ny, fx + nx * fy, peers

    greet([up, down, near, far] + [dev for g in plan for _, dev in members(*g)[2]])

    slot = [0]
    pending = []

    def send(src, dst, device):
        copy = remote(src, dst, sems, slot[0], device)
        slot[0] += 1
        copy.start()
        pending.append(copy)
        return copy

    state = [{"off": 0, "n": extent, "src": sums, "box": 0} for _ in chunks]
    history = [[] for _ in chunks]
    flight = {}

    def rws(at, n):
        return pl.ds(pl.multiple_of(at, SUB), n)

    def rs(step, c):
        lo, hi = chunks[c]
        s = state[c]
        size, mine, peers = members(*plan[step])
        split = step < 3
        n = s["n"] // size if split else s["n"]
        copies = []
        for field, device in peers:
            give = s["off"] + field * n if split else s["off"]
            box = s["box"] + mine * n
            copies.append(send(s["src"].at[lo:hi, rws(give, n), :], inbox.at[lo:hi, rws(box, n), :], device))
        keep = s["off"] + mine * n if split else s["off"]
        history[c].append((size, mine, peers, split))
        flight["rs", step, c] = (copies, keep, n, size, mine, [f for f, _ in peers], s["box"], split)
        s["box"] += size * n

    def rse(step, c):
        lo, hi = chunks[c]
        copies, keep, n, size, mine, fields, box, split = flight.pop(("rs", step, c))
        s = state[c]
        for copy in copies:
            copy.wait_recv()
        own = s["src"][lo:hi, rws(keep, n), :]
        if split:
            total = own
            for f in fields:
                total += inbox[lo:hi, rws(box + f * n, n), :]
        else:
            inbox[lo:hi, rws(box + mine * n, n), :] = own
            total = inbox[lo:hi, rws(box, n), :]
            for j in range(1, size):
                total += inbox[lo:hi, rws(box + j * n, n), :]
        part[step, lo:hi, rws(keep, n), :] = total
        s["off"], s["n"], s["src"] = keep, n, part.at[step]

    def div(c):
        lo, hi = chunks[c]
        first = 1 if lo == 0 else 0
        s = state[c]
        keep = rws(s["off"], s["n"])
        weight = s["src"][0, keep, :] + 1e-05
        for k in range(lo + first, hi):
            out_probe[k - 1, keep, :] = s["src"][k, keep, :] / weight

    def planes_of(c):
        lo, hi = chunks[c][:2]
        return max(lo - 1, 0), hi - 1

    def give(c, off, n, device):
        lo, hi = planes_of(c)
        own = out_probe.at[lo:hi, rws(off, n), :]
        return send(own, own, device)

    def agz(c):
        off, n = state[c]["off"], state[c]["n"]
        _, _, z_peers, _ = history[c][2]
        _, _, p_peers, _ = history[c][1]
        zs = [give(c, off, n, device) for _, device in z_peers]
        ps = [[give(c, off, n, device)] for _, device in p_peers]
        flight["agz", c] = (zs, ps)

    def agp(c):
        off, n = state[c]["off"], state[c]["n"]
        z_size, z_mine, z_peers, _ = history[c][2]
        _, _, p_peers, _ = history[c][1]
        _, _, ((_, partner),), _ = history[c][0]
        zs, ps = flight.pop(("agz", c))
        base = off - z_mine * n
        for (field, _), copy in zip(z_peers, zs):
            copy.wait_recv()
            for (_, device), got in zip(p_peers, ps):
                got.append(give(c, base + field * n, n, device))
        flight["agp", c] = (ps, base, n * z_size, [give(c, base, n * z_size, partner)])

    def agc(c):
        ps, base, n, cs = flight.pop(("agp", c))
        p_size, p_mine, p_peers, _ = history[c][1]
        _, _, ((_, partner),), _ = history[c][0]
        for (field, _), copies in zip(p_peers, ps):
            for copy in copies:
                copy.wait_recv()
            cs.append(give(c, base + (field - p_mine) * n, n, partner))
        flight["agc", c] = cs

    def age(c):
        for copy in flight.pop(("agc", c)):
            copy.wait_recv()

    band_at = (0, m + rows)
    piece = m // PIECES

    def corner(side, b, i):
        band = pl.ds(band_at[b] + i * piece, piece)
        flight["corner", side, b, i] = send(
            acc.at[:, pl.ds(halo_at[side], mt), band, :], came[side].at[:, :, band, :], sides[side]
        )

    def mid(side, i, of):
        band = pl.ds(m + i * (rows // of), rows // of)
        flight["mid", side, i] = send(
            acc.at[:, pl.ds(halo_at[side], mt), band, :], came[side].at[:, :, band, :], sides[side]
        )

    def vert(side, b, i):
        flight.pop(("corner", side, b, i)).wait_recv()
        band = pl.ds(band_at[b] + i * piece, piece)
        here = pl.ds(i * piece, piece)
        own = acc[:, pl.ds(half_at[side], mt), band, :]
        vsend[b, side, :, :, here, :] = own + came[side][:, :, band, :]
        flight["vert", side, b, i] = send(
            vsend.at[b, side, :, :, here, :], vrecv.at[b, side, :, :, here, :], (up, down)[b]
        )

    power_box = []
    def power():
        total = jnp.zeros((extent, extent), F32)
        for k in range(modes):
            for c in range(2):
                total += probe[k, c] * probe[k, c]
        power_box.append(jnp.max(total, keepdims=True) + 1e-06)

    def finish():
        scale = power_box[0]
        for key in [k for k in flight if k[0] in ("mid", "vert")]:
            flight.pop(key).wait_recv()
        for side in range(2):
            for t in range(mt):
                dst = pl.ds(pl.multiple_of((half_at[side] - mt + t) * LANE, LANE), LANE)
                for c in range(2):
                    base = acc[c, half_at[side] + t, pl.ds(m, rows), :] + came[side][c, t, pl.ds(m, rows), :]
                    ends = jnp.concatenate([vrecv[1, side, c, t], vrecv[0, side, c, t]], 0)
                    out_obj[c, :, dst] = (base + ends) / scale

    ops = {"rs": rs, "rse": rse, "div": div, "agz": agz, "agp": agp, "agc": agc, "age": age, "corner": corner, "mid": mid, "vert": vert, "power": power, "finish": finish}
    for name, *args in fold_schedule(steps, len(chunks)):
        ops[name](*args)
    assert not flight, flight
    for copy in pending:
        copy.wait_send()


def body(n_gx, n_gy, object_field, probe_field, amplitude, offsets):
    extent = probe_field.shape[-1]
    modes = probe_field.shape[0]
    margin = extent // 2
    rows, cols = object_field.shape[1:]
    mt, ct = margin // LANE, cols // LANE
    ext_shape = (2, 2 * mt + ct, rows + 2 * margin, LANE)
    ext = pl.pallas_call(
        functools.partial(halo_kernel, n_gx, n_gy, margin),
        out_shape=jax.ShapeDtypeStruct(ext_shape, F32),
        in_specs=[HBM],
        out_specs=VMEM,
        scratch_shapes=[pltpu.SemaphoreType.DMA((2, (2 + 8 * STRIPS) * mt)), pltpu.SemaphoreType.DMA((ct,))],
        compiler_params=pltpu.CompilerParams(collective_id=0, has_side_effects=True, vmem_limit_bytes=LIMIT),
        name="halo",
    )(object_field)

    planes = 2 * modes + 1
    acc, sums = pl.pallas_call(
        functools.partial(update_kernel, margin),
        out_shape=(
            jax.ShapeDtypeStruct(ext_shape, F32),
            jax.ShapeDtypeStruct((planes, extent, extent), F32),
        ),
        in_specs=[
            pl.BlockSpec(memory_space=pltpu.SMEM),
            VMEM,
            VMEM,
            VMEM,
            VMEM,
        ],
        out_specs=(VMEM, VMEM),
        scratch_shapes=[
            pltpu.VMEM((2, 2, extent, extent), F32),
            pltpu.VMEM((2, modes, 2, extent, extent), F32),
            pltpu.VMEM((2, 2 * extent, modes * extent), BF16),
            pltpu.VMEM((modes * extent, 2 * extent), BF16),
            pltpu.VMEM((2, modes * extent, 2 * extent), F32),
            pltpu.VMEM((2 * extent, 2 * extent), BF16),
            pltpu.VMEM((2 * extent, 2 * extent), BF16),
        ],
        compiler_params=pltpu.CompilerParams(vmem_limit_bytes=LIMIT),
        name="update",
    )(offsets.transpose(1, 2, 0), ext, probe_field, amplitude[:, 0], dft_tables(extent))

    plan = reduce_plan(n_gx, n_gy)
    peers = sum((1 << (cx + cy)) - 1 for _, cx, _, cy in plan)
    chunks = ((0, modes + 1), (modes + 1, planes))
    out_obj, out_probe = pl.pallas_call(
        functools.partial(fold_kernel, n_gx, n_gy, margin, chunks),
        out_shape=(
            jax.ShapeDtypeStruct(object_field.shape, F32),
            jax.ShapeDtypeStruct((2 * modes, extent, extent), F32),
        ),
        in_specs=[VMEM] * 3,
        out_specs=(VMEM, VMEM),
        scratch_shapes=[
            pltpu.VMEM((2, mt, rows + 2 * margin, LANE), F32),
            pltpu.VMEM((2, mt, rows + 2 * margin, LANE), F32),
            pltpu.VMEM((2, 2, 2, mt, margin, LANE), F32),
            pltpu.VMEM((2, 2, 2, mt, margin, LANE), F32),
            pltpu.VMEM((len(plan), planes, extent, extent), F32),
            pltpu.VMEM((planes, 3 * extent, extent), F32),
            pltpu.SemaphoreType.DMA((2, 8 * PIECES + 2 * MIDS + (peers + 24) * len(chunks))),
        ],
        compiler_params=pltpu.CompilerParams(
            collective_id=1, has_side_effects=True, vmem_limit_bytes=LIMIT
        ),
        name="fold",
    )(acc, probe_field, sums)
    return object_field + out_obj, probe_field + out_probe.reshape(probe_field.shape)


def solution(mesh):
    in_specs = (P(None, "gx", "gy"), P(), P("gx", "gy", None, None), P("gx", "gy", None))
    out_specs = (P(None, "gx", "gy"), P())
    step = functools.partial(body, mesh.shape["gx"], mesh.shape["gy"])
    return jax.shard_map(step, mesh=mesh, in_specs=in_specs, out_specs=out_specs, check_vma=False)
```

```python
import functools
import math

import jax
import jax.numpy as jnp
import numpy as np
from jax import lax
from jax.experimental import pallas as pl
from jax.experimental.pallas import tpu as pltpu
from jax.sharding import PartitionSpec as P

MESH = pl.DeviceIdType.MESH
VMEM = pl.BlockSpec(memory_space=pltpu.VMEM)
HBM = pl.BlockSpec(memory_space=pltpu.MemorySpace.HBM)
F32 = jnp.float32
BF16 = jnp.bfloat16
CHUNK = 32
SUB = 8
LANE = 128
STRIPS = 2
PIECES = 2
MIDS = 2
LIMIT = 8 << 20
STEP_LIMIT = 40 << 20


def dft_tables(extent):
    indices = np.arange(extent)
    angles = (indices[:, None] * indices[None, :] % extent) * (2.0 * math.pi / extent)
    norm_factor = 1.0 / math.sqrt(extent)
    both = np.concatenate([np.cos(angles), np.sin(angles)], 1) * norm_factor
    return jnp.asarray(both.astype(np.float32).astype(jnp.bfloat16))


def remote(src, dst, sems, slot, device):
    return pltpu.make_async_remote_copy(
        src_ref=src,
        dst_ref=dst,
        send_sem=sems.at[0, slot],
        recv_sem=sems.at[1, slot],
        device_id=device,
        device_id_type=MESH,
    )


def greet(devices):
    barrier = pltpu.get_barrier_semaphore()
    for device in devices:
        pl.semaphore_signal(barrier, inc=1, device_id=device, device_id_type=MESH)
    pl.semaphore_wait(barrier, len(devices))


def halo_kernel(n_gx, n_gy, margin, obj, ext, sems, local_sem):
    gx, gy = lax.axis_index("gx"), lax.axis_index("gy")
    rows, cols = obj.shape[1], obj.shape[2]
    m = margin
    mt, ct = m // LANE, cols // LANE
    odd = lax.rem(gy, 2)
    up = (lax.rem(gx + n_gx - 1, n_gx), gy)
    down = (lax.rem(gx + 1, n_gx), gy)
    step_y = 1 - 2 * odd
    near = (gx, gy + step_y)
    far = (gx, lax.rem(gy - step_y + n_gy, n_gy))
    sides = (near, far)
    half_at = ((1 - odd) * (ct - mt), odd * (ct - mt))
    lands_at = (odd * (mt + ct), (1 - odd) * (mt + ct))
    owns = [
        pltpu.make_async_copy(
            obj.at[:, :, pl.ds(t * LANE, LANE)], ext.at[:, mt + t, pl.ds(m, rows), :], local_sem.at[t]
        )
        for t in range(ct)
    ]
    for own in owns:
        own.start()
    greet((up, down, near, far))
    slot = [0]
    pending = []

    def send(src, dst, device):
        copy = remote(src, dst, sems, slot[0], device)
        slot[0] += 1
        copy.start()
        pending.append(copy)
        return copy

    piece = m // STRIPS
    ways = ((0, m + rows, up), (rows - m, 0, down))
    arrivals = []
    waits = []

    def lanes(side, t):
        return pl.ds(pl.multiple_of((half_at[side] + t) * LANE, LANE), LANE)

    def middle(side):
        for t in range(mt):
            dst = ext.at[:, lands_at[side] + t, pl.ds(m, rows), :]
            waits.append(send(obj.at[:, :, lanes(side, t)], dst, sides[side]))

    def vertical(side):
        for i in range(STRIPS):
            for src_row, dst_row, device in ways:
                band = pl.ds(dst_row + i * piece, piece)
                for t in range(mt):
                    src = obj.at[:, pl.ds(src_row + i * piece, piece), lanes(side, t)]
                    dst = ext.at[:, mt + half_at[side] + t, band, :]
                    arrivals.append((send(src, dst, device), side, band, t))

    vertical(1)
    middle(1)
    vertical(0)
    middle(0)
    for copy, side, band, t in arrivals:
        copy.wait_recv()
        src = ext.at[:, mt + half_at[side] + t, band, :]
        waits.append(send(src, ext.at[:, lands_at[side] + t, band, :], sides[side]))
    for copy in waits:
        copy.wait_recv()
    for copy in pending:
        copy.wait_send()
    for own in owns:
        own.wait()


def reduce_plan(n_gx, n_gy):
    x_bits, y_bits = n_gx.bit_length() - 1, n_gy.bit_length() - 1
    steps = [(0, 0, 0, 1), (0, 1, 1, 1)]
    steps.append((1, min(2, x_bits - 1), 0, 0))
    for b in range(3, x_bits, 2):
        steps.append((b, min(2, x_bits - b), 0, 0))
    for b in range(2, y_bits, 2):
        steps.append((0, 0, b, min(2, y_bits - b)))
    return steps


def step_kernel(n_gx, n_gy, margin, offs, ext, probe, amp, table, out_obj, out_probe, *scratch):
    (win, psi, xbuf, ybuf, ffwd, yback, fback, half, fr, frt, pads, acc, sums) = scratch[:13]
    (from_near, from_far, vsend, vrecv, part, inbox, sems) = scratch[13:]
    positions = amp.shape[0]
    gx, gy = lax.axis_index("gx"), lax.axis_index("gy")
    rows, cols = out_obj.shape[1], out_obj.shape[2]
    planes, extent = sums.shape[0], sums.shape[1]
    modes = probe.shape[0]
    m = margin
    mt, ct = m // LANE, cols // LANE
    odd = lax.rem(gy, 2)
    up = (lax.rem(gx + n_gx - 1, n_gx), gy)
    down = (lax.rem(gx + 1, n_gx), gy)
    step_y = 1 - 2 * odd
    near = (gx, gy + step_y)
    far = (gx, lax.rem(gy - step_y + n_gy, n_gy))
    sides = (near, far)
    came = (from_near, from_far)
    halo_at = ((1 - odd) * (mt + ct), odd * (mt + ct))
    half_at = (mt + (1 - odd) * (ct - mt), mt + odd * (ct - mt))
    plan = reduce_plan(n_gx, n_gy)
    steps = len(plan)
    chunks = [(0, 1)] + [(2 * i + 1, 2 * i + 3) for i in range(modes)]

    def swap(field, d, bits):
        out = 0
        for b in range(bits):
            bit = lax.rem(field // (1 << b), 2)
            out = out + (1 << b) * (1 - bit if d >> b & 1 else bit)
        return out

    def members(bx, cx, by, cy):
        nx, ny = 1 << cx, 1 << cy
        fx, fy = lax.rem(gx // (1 << bx), nx), lax.rem(gy // (1 << by), ny)
        peers = []
        for dy in range(ny):
            for dx in range(nx):
                if dx or dy:
                    px, py = swap(fx, dx, cx), swap(fy, dy, cy)
                    peers.append((px + nx * py, (gx + (px - fx) * (1 << bx), gy + (py - fy) * (1 << by))))
        return nx * ny, fx + nx * fy, peers

    friends = [up, down, near, far] + [dev for g in plan for _, dev in members(*g)[2]]
    barrier = pltpu.get_barrier_semaphore()
    for device in friends:
        pl.semaphore_signal(barrier, inc=1, device_id=device, device_id_type=MESH)

    slot = [0]
    pending = []

    def send(src, dst, device):
        copy = remote(src, dst, sems, slot[0], device)
        slot[0] += 1
        copy.start()
        pending.append(copy)
        return copy

    state = [{"off": 0, "n": extent, "src": sums, "box": 0} for _ in chunks]
    history = [[] for _ in chunks]
    flight = {}

    def rws(at, n):
        return pl.ds(pl.multiple_of(at, SUB), n)

    def rs(step, c):
        lo, hi = chunks[c]
        s = state[c]
        size, mine, peers = members(*plan[step])
        split = step < 3
        n = s["n"] // size if split else s["n"]
        copies = []
        for field, device in peers:
            give = s["off"] + field * n if split else s["off"]
            box = s["box"] + mine * n
            copies.append(send(s["src"].at[lo:hi, rws(give, n), :], inbox.at[lo:hi, rws(box, n), :], device))
        keep = s["off"] + mine * n if split else s["off"]
        history[c].append((size, mine, peers, split))
        flight["rs", step, c] = (copies, keep, n, size, mine, [f for f, _ in peers], s["box"], split)
        s["box"] += size * n

    def rse(step, c):
        lo, hi = chunks[c]
        copies, keep, n, size, mine, fields, box, split = flight.pop(("rs", step, c))
        s = state[c]
        for copy in copies:
            copy.wait_recv()
        own = s["src"][lo:hi, rws(keep, n), :]
        if split:
            total = own
            for f in fields:
                total += inbox[lo:hi, rws(box + f * n, n), :]
        else:
            inbox[lo:hi, rws(box + mine * n, n), :] = own
            total = inbox[lo:hi, rws(box, n), :]
            for j in range(1, size):
                total += inbox[lo:hi, rws(box + j * n, n), :]
        part[step, lo:hi, rws(keep, n), :] = total
        s["off"], s["n"], s["src"] = keep, n, part.at[step]

    def div(c):
        lo, hi = chunks[c]
        first = 1 if lo == 0 else 0
        s = state[c]
        keep = rws(s["off"], s["n"])
        weight = s["src"][0, keep, :] + 1e-05
        for k in range(lo + first, hi):
            out_probe[k - 1, keep, :] = s["src"][k, keep, :] / weight

    def planes_of(c):
        lo, hi = chunks[c][:2]
        return max(lo - 1, 0), hi - 1

    def give(c, off, n, device):
        lo, hi = planes_of(c)
        own = out_probe.at[lo:hi, rws(off, n), :]
        return send(own, own, device)

    def agz(c):
        off, n = state[c]["off"], state[c]["n"]
        _, _, z_peers, _ = history[c][2]
        _, _, p_peers, _ = history[c][1]
        zs = [give(c, off, n, device) for _, device in z_peers]
        ps = [[give(c, off, n, device)] for _, device in p_peers]
        flight["agz", c] = (zs, ps)

    def agp(c):
        off, n = state[c]["off"], state[c]["n"]
        z_size, z_mine, z_peers, _ = history[c][2]
        _, _, p_peers, _ = history[c][1]
        _, _, ((_, partner),), _ = history[c][0]
        zs, ps = flight.pop(("agz", c))
        base = off - z_mine * n
        for (field, _), copy in zip(z_peers, zs):
            copy.wait_recv()
            for (_, device), got in zip(p_peers, ps):
                got.append(give(c, base + field * n, n, device))
        flight["agp", c] = (ps, base, n * z_size, [give(c, base, n * z_size, partner)])

    def agc(c):
        ps, base, n, cs = flight.pop(("agp", c))
        p_size, p_mine, p_peers, _ = history[c][1]
        _, _, ((_, partner),), _ = history[c][0]
        for (field, _), copies in zip(p_peers, ps):
            for copy in copies:
                copy.wait_recv()
            cs.append(give(c, base + (field - p_mine) * n, n, partner))
        flight["agc", c] = cs

    def age(c):
        for copy in flight.pop(("agc", c)):
            copy.wait_recv()

    band_at = (0, m + rows)
    piece = m // PIECES

    def corner(side, b, i):
        band = pl.ds(band_at[b] + i * piece, piece)
        flight["corner", side, b, i] = send(
            acc.at[:, pl.ds(halo_at[side], mt), band, :], came[side].at[:, :, band, :], sides[side]
        )

    def mid(side, i, of):
        band = pl.ds(m + i * (rows // of), rows // of)
        flight["mid", side, i] = send(
            acc.at[:, pl.ds(halo_at[side], mt), band, :], came[side].at[:, :, band, :], sides[side]
        )

    def vert(side, b, i):
        flight.pop(("corner", side, b, i)).wait_recv()
        band = pl.ds(band_at[b] + i * piece, piece)
        here = pl.ds(i * piece, piece)
        own = acc[:, pl.ds(half_at[side], mt), band, :]
        vsend[b, side, :, :, here, :] = own + came[side][:, :, band, :]
        flight["vert", side, b, i] = send(
            vsend.at[b, side, :, :, here, :], vrecv.at[b, side, :, :, here, :], (up, down)[b]
        )

    power_box = []
    def power():
        total = jnp.zeros((extent, extent), F32)
        for k in range(modes):
            for c in range(2):
                total += probe[k, c] * probe[k, c]
        power_box.append(jnp.max(total, keepdims=True) + 1e-06)

    def finish():
        scale = power_box[0]
        for key in [k for k in flight if k[0] in ("mid", "vert")]:
            flight.pop(key).wait_recv()
        for side in range(2):
            for t in range(mt):
                dst = pl.ds(pl.multiple_of((half_at[side] - mt + t) * LANE, LANE), LANE)
                for c in range(2):
                    base = acc[c, half_at[side] + t, pl.ds(m, rows), :] + came[side][c, t, pl.ds(m, rows), :]
                    ends = jnp.concatenate([vrecv[1, side, c, t], vrecv[0, side, c, t]], 0)
                    out_obj[c, :, dst] = (base + ends) / scale

    starts = range(0, extent, CHUNK)

    last = ext.shape[1] - extent // LANE - 1
    c, s = table[:, :extent], table[:, extent:]
    fr[:extent, :extent] = c
    fr[:extent, extent:] = s
    fr[extent:, :extent] = -s
    fr[extent:, extent:] = c
    frt[:extent, :extent] = c
    frt[:extent, extent:] = -s
    frt[extent:, :extent] = s
    frt[extent:, extent:] = c

    lane = lax.broadcasted_iota(jnp.int32, (CHUNK, LANE), 1)

    def place(p):
        c0 = offs[0, 1, p] + margin
        tile = jnp.minimum(c0 // LANE, last)
        return offs[0, 0, p] + margin, tile, c0 - tile * LANE

    def add(plane, here, value, p):
        if p == 0:
            sums[plane, here, :] = value
        else:
            sums[plane, here, :] += value

    def extract(p, rb):
        r0, tile, low = place(p)
        here = pl.ds(rb, CHUNK)
        w = []
        for c in range(2):
            line = [
                pltpu.roll(ext[c, tile + t, pl.ds(r0 + rb, CHUNK), :], lax.rem(LANE - low, LANE), 1)
                for t in range(extent // LANE + 1)
            ]
            line = [jnp.where(lane < LANE - low, a, b) for a, b in zip(line, line[1:])]
            w.append(jnp.concatenate(line, 1))
            win[p, c, here, :] = w[c]
        add(0, here, w[0] * w[0] + w[1] * w[1], p)
        for k in range(modes):
            cols = slice(k * extent, (k + 1) * extent)
            pr, pi = probe[k, 0, here, :], probe[k, 1, here, :]
            psi_re = pr * w[0] - pi * w[1]
            psi_im = pr * w[1] + pi * w[0]
            psi[p, k, 0, here, :] = psi_re
            psi[p, k, 1, here, :] = psi_im
            xbuf[p, here, cols] = psi_re.astype(BF16)
            xbuf[p, pl.ds(extent + rb, CHUNK), cols] = psi_im.astype(BF16)

    def rows_pass(p, c):
        band = fr[c * extent : (c + 1) * extent, :]
        out = jnp.dot(band, xbuf[p], preferred_element_type=F32).astype(BF16)
        for k in range(modes):
            ybuf[k * extent : (k + 1) * extent, c * extent : (c + 1) * extent] = out[
                :, k * extent : (k + 1) * extent
            ]

    def cols_pass(p, k):
        band = slice(k * extent, (k + 1) * extent)
        ffwd[p % 2, band, :] = jnp.dot(ybuf[band, :], frt[...], preferred_element_type=F32)

    def rows_back(k, p, c):
        band = frt[c * extent : (c + 1) * extent, :]
        cols = slice(k * extent, (k + 1) * extent)
        out = jnp.dot(band, xbuf[p, :, cols], preferred_element_type=F32)
        yback[p % 2, :, c * extent : (c + 1) * extent] = out.astype(BF16)

    def cols_back(k, p):
        fback[p % 2] = jnp.dot(yback[p % 2], fr[...], preferred_element_type=F32)

    def project(p, rb):
        q = p % 2
        parts = []
        intensity = jnp.zeros((CHUNK, extent), F32)
        for k in range(modes):
            at = pl.ds(k * extent + rb, CHUNK)
            re, im = ffwd[q, at, :extent], ffwd[q, at, extent:]
            intensity += re * re + im * im
            parts.append((re, im))
        factor = amp[p, pl.ds(rb, CHUNK), :] * jnp.minimum(lax.rsqrt(intensity), 4.0)
        for k in range(modes):
            cols = slice(k * extent, (k + 1) * extent)
            xbuf[p, pl.ds(rb, CHUNK), cols] = (parts[k][0] * factor).astype(BF16)
            xbuf[p, pl.ds(extent + rb, CHUNK), cols] = (parts[k][1] * factor).astype(BF16)

    def correct(k, p, rb):
        here = pl.ds(rb, CHUNK)
        wr, wi = win[p, 0, here, :], win[p, 1, here, :]
        dr = fback[p % 2, here, :extent] - psi[p, k, 0, here, :]
        di = fback[p % 2, here, extent:] - psi[p, k, 1, here, :]
        pr, pi = probe[k, 0, here, :], probe[k, 1, here, :]
        add(2 * k + 1, here, wr * dr + wi * di, p)
        add(2 * k + 2, here, wr * di - wi * dr, p)
        value = [pr * dr + pi * di, pr * di - pi * dr]
        if k:
            value = [half[p, c, here, :] + value[c] for c in range(2)]
        if k + 1 < modes:
            for c in range(2):
                half[p, c, here, :] = value[c]
            return
        _, _, low = place(p)
        blank = jnp.zeros((CHUNK, LANE), F32)
        for c in range(2):
            line = [
                pltpu.roll(value[c][:, t * LANE : (t + 1) * LANE], lax.rem(low, LANE), 1)
                for t in range(extent // LANE)
            ]
            for t, (a, b) in enumerate(zip([blank] + line, line + [blank])):
                pads[p, c, t, pl.ds(CHUNK + rb, CHUNK), :] = jnp.where(lane < low, a, b)

    def blank_pads(p):
        for at in (0, CHUNK + extent):
            pads[p, :, :, at : at + CHUNK, :] = jnp.zeros((2, pads.shape[2], CHUNK, LANE), F32)

    def gather(lo, hi):
        tiles = pads.shape[2]
        for at in range(lo, hi, CHUNK):
            for t in range(acc.shape[1]):
                spots = []
                for p in range(positions):
                    r0, tile, _ = place(p)
                    row = jnp.clip(at - r0, -CHUNK, extent) + CHUNK
                    inside = (t >= tile) & (t < tile + tiles)
                    spots.append((p, jnp.clip(t - tile, 0, tiles - 1), jnp.where(inside, row, 0)))
                for c in range(2):
                    total = None
                    for p, tile, row in spots:
                        value = pads[p, c, tile, pl.ds(row, CHUNK), :]
                        total = value if total is None else total + value
                    acc[c, t, at : at + CHUNK, :] = total

    def beside(matmuls, others):
        n = len(matmuls)
        for i, (call, args) in enumerate(matmuls):
            call(*args)
            for other, rest in others[i * len(others) // n : (i + 1) * len(others) // n]:
                other(*rest)

    for rb in starts:
        extract(0, rb)
    for p in range(positions):
        beside(
            [(rows_pass, (p, 0)), (rows_pass, (p, 1))] + [(cols_pass, (p, k)) for k in range(modes)],
            [(blank_pads, (p,))]
            + ([(project, (p - 1, rb)) for rb in starts] if p else [])
            + ([(extract, (p + 1, rb)) for rb in starts] if p + 1 < positions else []),
        )
    for rb in starts:
        project(positions - 1, rb)
    pl.semaphore_wait(barrier, len(friends))
    rs(0, 0)

    def back(k, p):
        return [(rows_back, (k, p, 0)), (rows_back, (k, p, 1)), (cols_back, (k, p))]

    units = [(k, p) for k in range(modes) for p in range(positions)]
    beside(back(*units[0]), [])
    for u, (k, p) in enumerate(units):
        rest = [(correct, (k, p, rb)) for rb in starts]
        if u + 1 < len(units):
            beside(back(*units[u + 1]), rest)
        else:
            for call, args in rest:
                call(*args)
        if u == 2:
            rse(0, 0)
            rs(1, 0)
        if p + 1 == positions:
            rs(0, 1 + k)

    bands = [(b, i) for i in range(PIECES) for b in (0, 1)]

    def corners(side):
        for b, i in bands:
            corner(side, b, i)

    n = len(chunks)
    for c in range(1, n - 1):
        rse(0, c)
        rs(1, c)
    gather(0, m)
    gather(m + rows, m + rows + m)
    corners(0)
    rse(1, 0)
    rs(2, 0)
    rse(0, n - 1)
    rs(1, n - 1)
    corners(1)
    gather(m, m + rows)
    power()
    for b, i in bands:
        vert(0, b, i)
    for c in range(1, n):
        rse(1, c)
        rs(2, c)
    for side in (1, 0):
        for i in range(MIDS):
            mid(side, i, MIDS)
    for b, i in bands[: len(bands) // 2]:
        vert(1, b, i)
    for s in range(2, steps):
        for c in range(n):
            rse(s, c)
            if s + 1 < steps:
                rs(s + 1, c)
            elif c:
                div(c)
                agz(c)
    for b, i in bands[len(bands) // 2 :]:
        vert(1, b, i)
    for act in (agp, agc, age):
        for c in range(1, n):
            act(c)
    finish()
    assert not flight
    for copy in pending:
        copy.wait_send()


def body(n_gx, n_gy, object_field, probe_field, amplitude, offsets):
    extent = probe_field.shape[-1]
    modes = probe_field.shape[0]
    margin = extent // 2
    rows, cols = object_field.shape[1:]
    positions = amplitude.shape[0]
    mt, ct = margin // LANE, cols // LANE
    ext_shape = (2, 2 * mt + ct, rows + 2 * margin, LANE)
    ext = pl.pallas_call(
        functools.partial(halo_kernel, n_gx, n_gy, margin),
        out_shape=jax.ShapeDtypeStruct(ext_shape, F32),
        in_specs=[HBM],
        out_specs=VMEM,
        scratch_shapes=[pltpu.SemaphoreType.DMA((2, (2 + 8 * STRIPS) * mt)), pltpu.SemaphoreType.DMA((ct,))],
        compiler_params=pltpu.CompilerParams(collective_id=0, has_side_effects=True, vmem_limit_bytes=LIMIT),
        name="halo",
    )(object_field)

    planes = 2 * modes + 1
    plan = reduce_plan(n_gx, n_gy)
    peers = sum((1 << (cx + cy)) - 1 for _, cx, _, cy in plan)
    out_obj, out_probe = pl.pallas_call(
        functools.partial(step_kernel, n_gx, n_gy, margin),
        out_shape=(
            jax.ShapeDtypeStruct(object_field.shape, F32),
            jax.ShapeDtypeStruct((2 * modes, extent, extent), F32),
        ),
        in_specs=[pl.BlockSpec(memory_space=pltpu.SMEM), VMEM, VMEM, VMEM, VMEM],
        out_specs=(VMEM, VMEM),
        scratch_shapes=[
            pltpu.VMEM((positions, 2, extent, extent), F32),
            pltpu.VMEM((positions, modes, 2, extent, extent), F32),
            pltpu.VMEM((positions, 2 * extent, modes * extent), BF16),
            pltpu.VMEM((modes * extent, 2 * extent), BF16),
            pltpu.VMEM((2, modes * extent, 2 * extent), F32),
            pltpu.VMEM((2, extent, 2 * extent), BF16),
            pltpu.VMEM((2, extent, 2 * extent), F32),
            pltpu.VMEM((positions, 2, extent, extent), F32),
            pltpu.VMEM((2 * extent, 2 * extent), BF16),
            pltpu.VMEM((2 * extent, 2 * extent), BF16),
            pltpu.VMEM((positions, 2, extent // LANE + 1, extent + 2 * CHUNK, LANE), F32),
            pltpu.VMEM(ext_shape, F32),
            pltpu.VMEM((planes, extent, extent), F32),
            pltpu.VMEM((2, mt, rows + 2 * margin, LANE), F32),
            pltpu.VMEM((2, mt, rows + 2 * margin, LANE), F32),
            pltpu.VMEM((2, 2, 2, mt, margin, LANE), F32),
            pltpu.VMEM((2, 2, 2, mt, margin, LANE), F32),
            pltpu.VMEM((len(plan), planes, extent, extent), F32),
            pltpu.VMEM((planes, 2 * extent, extent), F32),
            pltpu.SemaphoreType.DMA((2, 8 * PIECES + 2 * MIDS + (peers + 24) * (modes + 1))),
        ],
        compiler_params=pltpu.CompilerParams(
            collective_id=1, has_side_effects=True, vmem_limit_bytes=STEP_LIMIT
        ),
        name="step",
    )(offsets.transpose(1, 2, 0), ext, probe_field, amplitude[:, 0], dft_tables(extent))
    return object_field + out_obj, probe_field + out_probe.reshape(probe_field.shape)


def solution(mesh):
    in_specs = (P(None, "gx", "gy"), P(), P("gx", "gy", None, None), P("gx", "gy", None))
    out_specs = (P(None, "gx", "gy"), P())
    step = functools.partial(body, mesh.shape["gx"], mesh.shape["gy"])
    return jax.shard_map(step, mesh=mesh, in_specs=in_specs, out_specs=out_specs, check_vma=False)
```

```python
import functools
import math

import jax
import jax.numpy as jnp
import numpy as np
from jax import lax
from jax.experimental import pallas as pl
from jax.experimental.pallas import tpu as pltpu
from jax.sharding import PartitionSpec as P

MESH = pl.DeviceIdType.MESH
VMEM = pl.BlockSpec(memory_space=pltpu.VMEM)
HBM = pl.BlockSpec(memory_space=pltpu.MemorySpace.HBM)
F32 = jnp.float32
BF16 = jnp.bfloat16
CHUNK = 32
SUB = 8
LANE = 128
STRIPS = 2
PIECES = 2
MIDS = 2
LIMIT = 8 << 20
STEP_LIMIT = 40 << 20


def dft_tables(extent):
    indices = np.arange(extent)
    angles = (indices[:, None] * indices[None, :] % extent) * (2.0 * math.pi / extent)
    norm_factor = 1.0 / math.sqrt(extent)
    both = np.concatenate([np.cos(angles), np.sin(angles)], 1) * norm_factor
    return jnp.asarray(both.astype(np.float32).astype(jnp.bfloat16))


def remote(src, dst, sems, slot, device):
    return pltpu.make_async_remote_copy(
        src_ref=src,
        dst_ref=dst,
        send_sem=sems.at[0, slot],
        recv_sem=sems.at[1, slot],
        device_id=device,
        device_id_type=MESH,
    )


def greet(devices):
    barrier = pltpu.get_barrier_semaphore()
    for device in devices:
        pl.semaphore_signal(barrier, inc=1, device_id=device, device_id_type=MESH)
    pl.semaphore_wait(barrier, len(devices))


def halo_kernel(n_gx, n_gy, margin, obj, ext, sems, local_sem):
    gx, gy = lax.axis_index("gx"), lax.axis_index("gy")
    rows, cols = obj.shape[1], obj.shape[2]
    m = margin
    mt, ct = m // LANE, cols // LANE
    odd = lax.rem(gy, 2)
    up = (lax.rem(gx + n_gx - 1, n_gx), gy)
    down = (lax.rem(gx + 1, n_gx), gy)
    step_y = 1 - 2 * odd
    near = (gx, gy + step_y)
    far = (gx, lax.rem(gy - step_y + n_gy, n_gy))
    sides = (near, far)
    half_at = ((1 - odd) * (ct - mt), odd * (ct - mt))
    lands_at = (odd * (mt + ct), (1 - odd) * (mt + ct))
    owns = [
        pltpu.make_async_copy(
            obj.at[:, :, pl.ds(t * LANE, LANE)], ext.at[:, mt + t, pl.ds(m, rows), :], local_sem.at[t]
        )
        for t in range(ct)
    ]
    for own in owns:
        own.start()
    greet((up, down, near, far))
    slot = [0]
    pending = []

    def send(src, dst, device):
        copy = remote(src, dst, sems, slot[0], device)
        slot[0] += 1
        copy.start()
        pending.append(copy)
        return copy

    piece = m // STRIPS
    ways = ((0, m + rows, up), (rows - m, 0, down))
    arrivals = []
    waits = []

    def lanes(side, t):
        return pl.ds(pl.multiple_of((half_at[side] + t) * LANE, LANE), LANE)

    def middle(side):
        for t in range(mt):
            dst = ext.at[:, lands_at[side] + t, pl.ds(m, rows), :]
            waits.append(send(obj.at[:, :, lanes(side, t)], dst, sides[side]))

    def vertical(side):
        for i in range(STRIPS):
            for src_row, dst_row, device in ways:
                band = pl.ds(dst_row + i * piece, piece)
                for t in range(mt):
                    src = obj.at[:, pl.ds(src_row + i * piece, piece), lanes(side, t)]
                    dst = ext.at[:, mt + half_at[side] + t, band, :]
                    arrivals.append((send(src, dst, device), side, band, t))

    vertical(1)
    middle(1)
    vertical(0)
    middle(0)
    for copy, side, band, t in arrivals:
        copy.wait_recv()
        src = ext.at[:, mt + half_at[side] + t, band, :]
        waits.append(send(src, ext.at[:, lands_at[side] + t, band, :], sides[side]))
    for copy in waits:
        copy.wait_recv()
    for copy in pending:
        copy.wait_send()
    for own in owns:
        own.wait()


def reduce_plan(n_gx, n_gy, kind):
    x_bits, y_bits = n_gx.bit_length() - 1, n_gy.bit_length() - 1
    steps = [(0, 0, 0, 1)]
    if kind == "x":
        steps += [(0, 1, 0, 0), (1, min(2, x_bits - 1), 1, 1)]
    else:
        steps += [(0, 0, 1, 1), (0, min(3, x_bits), 0, 0)]
    for b in range(3, x_bits, 2):
        steps.append((b, min(2, x_bits - b), 0, 0))
    for b in range(2, y_bits, 2):
        steps.append((0, 0, b, min(2, y_bits - b)))
    return steps


def reduce_chunks(modes):
    planes = 2 * modes + 1
    chunks = [(0, 1, "x", 0), (0, 1, "y", planes)]
    return chunks + [(2 * k + 1, 2 * k + 3, "xy"[k % 2], 2 * k + 1) for k in range(modes)]


def step_kernel(n_gx, n_gy, margin, offs, ext, obj, probe, amp, table, out_obj, out_probe, *scratch):
    (win, psi, xbuf, ybuf, ffwd, yback, fback, half, fr, frt, pads, acc, sums) = scratch[:13]
    (from_near, from_far, vsend, vrecv, part, inbox, sems) = scratch[13:]
    positions = amp.shape[0]
    gx, gy = lax.axis_index("gx"), lax.axis_index("gy")
    rows, cols = out_obj.shape[1], out_obj.shape[2]
    planes, extent = sums.shape[0], sums.shape[1]
    modes = probe.shape[0]
    m = margin
    mt, ct = m // LANE, cols // LANE
    odd = lax.rem(gy, 2)
    up = (lax.rem(gx + n_gx - 1, n_gx), gy)
    down = (lax.rem(gx + 1, n_gx), gy)
    step_y = 1 - 2 * odd
    near = (gx, gy + step_y)
    far = (gx, lax.rem(gy - step_y + n_gy, n_gy))
    sides = (near, far)
    came = (from_near, from_far)
    halo_at = ((1 - odd) * (mt + ct), odd * (mt + ct))
    half_at = (mt + (1 - odd) * (ct - mt), mt + odd * (ct - mt))
    plans = {kind: reduce_plan(n_gx, n_gy, kind) for kind in "xy"}
    steps = len(plans["x"])
    chunks = reduce_chunks(modes)

    def swap(field, d, bits):
        out = 0
        for b in range(bits):
            bit = lax.rem(field // (1 << b), 2)
            out = out + (1 << b) * (1 - bit if d >> b & 1 else bit)
        return out

    def members(bx, cx, by, cy):
        nx, ny = 1 << cx, 1 << cy
        fx, fy = lax.rem(gx // (1 << bx), nx), lax.rem(gy // (1 << by), ny)
        peers = []
        for dy in range(ny):
            for dx in range(nx):
                if dx or dy:
                    px, py = swap(fx, dx, cx), swap(fy, dy, cy)
                    peers.append((px + nx * py, (gx + (px - fx) * (1 << bx), gy + (py - fy) * (1 << by))))
        return nx * ny, fx + nx * fy, peers

    friends = [up, down, near, far] + [
        dev for plan in plans.values() for g in plan for _, dev in members(*g)[2]
    ]
    barrier = pltpu.get_barrier_semaphore()
    for device in friends:
        pl.semaphore_signal(barrier, inc=1, device_id=device, device_id_type=MESH)

    slot = [0]
    pending = []

    def send(src, dst, device):
        copy = remote(src, dst, sems, slot[0], device)
        slot[0] += 1
        copy.start()
        pending.append(copy)
        return copy

    state = [{"off": 0, "n": extent, "src": (sums, lo, hi), "box": 0} for lo, hi, _, _ in chunks]
    history = [[] for _ in chunks]
    flight = {}

    def rws(at, n):
        return pl.ds(pl.multiple_of(at, SUB), n)

    def slots(c):
        lo, hi, _, slot = chunks[c]
        return slice(slot, slot + hi - lo)

    def rs(step, c):
        s = state[c]
        size, mine, peers = members(*plans[chunks[c][2]][step])
        split = step < 3
        n = s["n"] // size if split else s["n"]
        src, lo, hi = s["src"]
        copies = []
        for field, device in peers:
            give = s["off"] + field * n if split else s["off"]
            box = inbox.at[slots(c), rws(s["box"] + mine * n, n), :]
            copies.append(send(src.at[lo:hi, rws(give, n), :], box, device))
        keep = s["off"] + mine * n if split else s["off"]
        history[c].append((size, mine, peers, split))
        flight["rs", step, c] = (copies, keep, n, size, mine, [f for f, _ in peers], s["box"], split)
        s["box"] += size * n

    def rse(step, c):
        at = slots(c)
        copies, keep, n, size, mine, fields, box, split = flight.pop(("rs", step, c))
        s = state[c]
        for copy in copies:
            copy.wait_recv()
        src, lo, hi = s["src"]
        own = src[lo:hi, rws(keep, n), :]
        if split:
            total = own
            for f in fields:
                total += inbox[at, rws(box + f * n, n), :]
        else:
            inbox[at, rws(box + mine * n, n), :] = own
            total = inbox[at, rws(box, n), :]
            for j in range(1, size):
                total += inbox[at, rws(box + j * n, n), :]
        part[step, at, rws(keep, n), :] = total
        s["off"], s["n"], s["src"] = keep, n, (part.at[step], at.start, at.stop)

    def follow(c, other):
        state[c] = dict(state[other], box=0)
        history[c] = list(history[other])

    def div(c):
        lo, hi, kind, slot = chunks[c]
        s = state[c]
        keep = rws(s["off"], s["n"])
        weight = part[steps - 1, slots("xy".index(kind)).start, keep, :] + 1e-05
        for k in range(lo, hi):
            mode, c = divmod(k - 1, 2)
            step = part[steps - 1, slot + k - lo, keep, :] / weight
            out_probe[k - 1, keep, :] = probe[mode, c, keep, :] + step

    def planes_of(c):
        lo, hi = chunks[c][:2]
        return max(lo - 1, 0), hi - 1

    def give(c, off, n, device):
        lo, hi = planes_of(c)
        own = out_probe.at[lo:hi, rws(off, n), :]
        return send(own, own, device)

    def agz(c):
        off, n = state[c]["off"], state[c]["n"]
        _, _, z_peers, _ = history[c][2]
        _, _, p_peers, _ = history[c][1]
        zs = [give(c, off, n, device) for _, device in z_peers]
        ps = [[give(c, off, n, device)] for _, device in p_peers]
        flight["agz", c] = (zs, ps)

    def agp(c):
        off, n = state[c]["off"], state[c]["n"]
        z_size, z_mine, z_peers, _ = history[c][2]
        _, _, p_peers, _ = history[c][1]
        _, _, ((_, partner),), _ = history[c][0]
        zs, ps = flight.pop(("agz", c))
        base = off - z_mine * n
        for (field, _), copy in zip(z_peers, zs):
            copy.wait_recv()
            for (_, device), got in zip(p_peers, ps):
                got.append(give(c, base + field * n, n, device))
        flight["agp", c] = (ps, base, n * z_size, [give(c, base, n * z_size, partner)])

    def agc(c):
        ps, base, n, cs = flight.pop(("agp", c))
        p_size, p_mine, p_peers, _ = history[c][1]
        _, _, ((_, partner),), _ = history[c][0]
        for (field, _), copies in zip(p_peers, ps):
            for copy in copies:
                copy.wait_recv()
            cs.append(give(c, base + (field - p_mine) * n, n, partner))
        flight["agc", c] = cs

    def age(c):
        for copy in flight.pop(("agc", c)):
            copy.wait_recv()

    band_at = (0, m + rows)
    piece = m // PIECES

    def corner(side, b, i):
        band = pl.ds(band_at[b] + i * piece, piece)
        flight["corner", side, b, i] = send(
            acc.at[:, pl.ds(halo_at[side], mt), band, :], came[side].at[:, :, band, :], sides[side]
        )

    def mid(side, i, of):
        band = pl.ds(m + i * (rows // of), rows // of)
        flight["mid", side, i] = send(
            acc.at[:, pl.ds(halo_at[side], mt), band, :], came[side].at[:, :, band, :], sides[side]
        )

    def vert(side, b, i):
        flight.pop(("corner", side, b, i)).wait_recv()
        band = pl.ds(band_at[b] + i * piece, piece)
        here = pl.ds(i * piece, piece)
        own = acc[:, pl.ds(half_at[side], mt), band, :]
        vsend[b, side, :, :, here, :] = own + came[side][:, :, band, :]
        flight["vert", side, b, i] = send(
            vsend.at[b, side, :, :, here, :], vrecv.at[b, side, :, :, here, :], (up, down)[b]
        )

    power_box = []
    def power():
        total = jnp.zeros((extent, extent), F32)
        for k in range(modes):
            for c in range(2):
                total += probe[k, c] * probe[k, c]
        power_box.append(jnp.max(total, keepdims=True) + 1e-06)

    def finish():
        scale = power_box[0]
        for key in [k for k in flight if k[0] in ("mid", "vert")]:
            flight.pop(key).wait_recv()
        for side in range(2):
            for t in range(mt):
                dst = pl.ds(pl.multiple_of((half_at[side] - mt + t) * LANE, LANE), LANE)
                for c in range(2):
                    base = acc[c, half_at[side] + t, pl.ds(m, rows), :] + came[side][c, t, pl.ds(m, rows), :]
                    ends = jnp.concatenate([vrecv[1, side, c, t], vrecv[0, side, c, t]], 0)
                    out_obj[c, :, dst] = obj[c, :, dst] + (base + ends) / scale

    starts = range(0, extent, CHUNK)

    last = ext.shape[1] - extent // LANE - 1
    c, s = table[:, :extent], table[:, extent:]
    fr[:extent, :extent] = c
    fr[:extent, extent:] = s
    fr[extent:, :extent] = -s
    fr[extent:, extent:] = c
    frt[:extent, :extent] = c
    frt[:extent, extent:] = -s
    frt[extent:, :extent] = s
    frt[extent:, extent:] = c

    lane = lax.broadcasted_iota(jnp.int32, (CHUNK, LANE), 1)

    def place(p):
        c0 = offs[0, 1, p] + margin
        tile = jnp.minimum(c0 // LANE, last)
        return offs[0, 0, p] + margin, tile, c0 - tile * LANE

    def add(plane, here, value, p):
        if p == 0:
            sums[plane, here, :] = value
        else:
            sums[plane, here, :] += value

    def extract(p, rb):
        r0, tile, low = place(p)
        here = pl.ds(rb, CHUNK)
        w = []
        for c in range(2):
            line = [
                pltpu.roll(ext[c, tile + t, pl.ds(r0 + rb, CHUNK), :], lax.rem(LANE - low, LANE), 1)
                for t in range(extent // LANE + 1)
            ]
            line = [jnp.where(lane < LANE - low, a, b) for a, b in zip(line, line[1:])]
            w.append(jnp.concatenate(line, 1))
            win[p, c, here, :] = w[c]
        add(0, here, w[0] * w[0] + w[1] * w[1], p)
        for k in range(modes):
            cols = slice(k * extent, (k + 1) * extent)
            pr, pi = probe[k, 0, here, :], probe[k, 1, here, :]
            psi_re = pr * w[0] - pi * w[1]
            psi_im = pr * w[1] + pi * w[0]
            psi[p, k, 0, here, :] = psi_re
            psi[p, k, 1, here, :] = psi_im
            xbuf[p, here, cols] = psi_re.astype(BF16)
            xbuf[p, pl.ds(extent + rb, CHUNK), cols] = psi_im.astype(BF16)

    def rows_pass(p, c):
        band = fr[c * extent : (c + 1) * extent, :]
        out = jnp.dot(band, xbuf[p], preferred_element_type=F32).astype(BF16)
        for k in range(modes):
            ybuf[k * extent : (k + 1) * extent, c * extent : (c + 1) * extent] = out[
                :, k * extent : (k + 1) * extent
            ]

    def cols_pass(p, k):
        band = slice(k * extent, (k + 1) * extent)
        ffwd[p % 2, band, :] = jnp.dot(ybuf[band, :], frt[...], preferred_element_type=F32)

    def rows_back(k, p, c):
        band = frt[c * extent : (c + 1) * extent, :]
        cols = slice(k * extent, (k + 1) * extent)
        out = jnp.dot(band, xbuf[p, :, cols], preferred_element_type=F32)
        yback[p % 2, :, c * extent : (c + 1) * extent] = out.astype(BF16)

    def cols_back(k, p):
        fback[p % 2] = jnp.dot(yback[p % 2], fr[...], preferred_element_type=F32)

    def project(p, rb):
        q = p % 2
        parts = []
        intensity = jnp.zeros((CHUNK, extent), F32)
        for k in range(modes):
            at = pl.ds(k * extent + rb, CHUNK)
            re, im = ffwd[q, at, :extent], ffwd[q, at, extent:]
            intensity += re * re + im * im
            parts.append((re, im))
        factor = amp[p, pl.ds(rb, CHUNK), :] * jnp.minimum(lax.rsqrt(intensity), 4.0)
        for k in range(modes):
            cols = slice(k * extent, (k + 1) * extent)
            xbuf[p, pl.ds(rb, CHUNK), cols] = (parts[k][0] * factor).astype(BF16)
            xbuf[p, pl.ds(extent + rb, CHUNK), cols] = (parts[k][1] * factor).astype(BF16)

    def correct(k, p, rb):
        here = pl.ds(rb, CHUNK)
        wr, wi = win[p, 0, here, :], win[p, 1, here, :]
        dr = fback[p % 2, here, :extent] - psi[p, k, 0, here, :]
        di = fback[p % 2, here, extent:] - psi[p, k, 1, here, :]
        pr, pi = probe[k, 0, here, :], probe[k, 1, here, :]
        add(2 * k + 1, here, wr * dr + wi * di, p)
        add(2 * k + 2, here, wr * di - wi * dr, p)
        value = [pr * dr + pi * di, pr * di - pi * dr]
        if k:
            value = [half[p, c, here, :] + value[c] for c in range(2)]
        if k + 1 < modes:
            for c in range(2):
                half[p, c, here, :] = value[c]
            return
        _, _, low = place(p)
        blank = jnp.zeros((CHUNK, LANE), F32)
        for c in range(2):
            line = [
                pltpu.roll(value[c][:, t * LANE : (t + 1) * LANE], lax.rem(low, LANE), 1)
                for t in range(extent // LANE)
            ]
            for t, (a, b) in enumerate(zip([blank] + line, line + [blank])):
                pads[p, c, t, pl.ds(CHUNK + rb, CHUNK), :] = jnp.where(lane < low, a, b)

    def blank_pads(p):
        for at in (0, CHUNK + extent):
            pads[p, :, :, at : at + CHUNK, :] = jnp.zeros((2, pads.shape[2], CHUNK, LANE), F32)

    def gather(lo, hi):
        tiles = pads.shape[2]
        for at in range(lo, hi, CHUNK):
            for t in range(acc.shape[1]):
                spots = []
                for p in range(positions):
                    r0, tile, _ = place(p)
                    row = jnp.clip(at - r0, -CHUNK, extent) + CHUNK
                    inside = (t >= tile) & (t < tile + tiles)
                    spots.append((p, jnp.clip(t - tile, 0, tiles - 1), jnp.where(inside, row, 0)))
                for c in range(2):
                    total = None
                    for p, tile, row in spots:
                        value = pads[p, c, tile, pl.ds(row, CHUNK), :]
                        total = value if total is None else total + value
                    acc[c, t, at : at + CHUNK, :] = total

    def beside(matmuls, others):
        n = len(matmuls)
        for i, (call, args) in enumerate(matmuls):
            call(*args)
            for other, rest in others[i * len(others) // n : (i + 1) * len(others) // n]:
                other(*rest)

    for rb in starts:
        extract(0, rb)
    for p in range(positions):
        beside(
            [(rows_pass, (p, 0)), (rows_pass, (p, 1))] + [(cols_pass, (p, k)) for k in range(modes)],
            [(blank_pads, (p,))]
            + ([(project, (p - 1, rb)) for rb in starts] if p else [])
            + ([(extract, (p + 1, rb)) for rb in starts] if p + 1 < positions else []),
        )
    for rb in starts:
        project(positions - 1, rb)
    pl.semaphore_wait(barrier, len(friends))
    rs(0, 0)

    def back(k, p):
        return [(rows_back, (k, p, 0)), (rows_back, (k, p, 1)), (cols_back, (k, p))]

    units = [(k, p) for k in range(modes) for p in range(positions)]
    beside(back(*units[0]), [])
    for u, (k, p) in enumerate(units):
        rest = [(correct, (k, p, rb)) for rb in starts]
        if u + 1 < len(units):
            beside(back(*units[u + 1]), rest)
        else:
            for call, args in rest:
                call(*args)
        if u == 2:
            rse(0, 0)
            follow(1, 0)
            rs(1, 0)
            rs(1, 1)
        if p + 1 == positions:
            rs(0, 2 + k)

    bands = [(b, i) for i in range(PIECES) for b in (0, 1)]
    half_way = len(bands) // 2
    early, late = range(2, len(chunks) - 1), len(chunks) - 1

    for c in early:
        rse(0, c)
        rs(1, c)
    gather(0, m)
    gather(m + rows, m + rows + m)
    for b, i in bands:
        corner(0, b, i)
    for c in (0, 1):
        rse(1, c)
        rs(2, c)
    rse(0, late)
    rs(1, late)
    for b, i in bands:
        corner(1, b, i)
    gather(m, m + rows)
    power()
    for b, i in bands[:half_way]:
        vert(0, b, i)
    for c in range(2, len(chunks)):
        rse(1, c)
        rs(2, c)
    for b, i in bands[half_way:]:
        vert(0, b, i)
    for side in (1, 0):
        for i in range(MIDS):
            mid(side, i, MIDS)
    for b, i in bands[:half_way]:
        vert(1, b, i)
    for s in range(2, steps):
        for c in range(len(chunks)):
            rse(s, c)
            if s + 1 < steps:
                rs(s + 1, c)
            elif c >= 2:
                div(c)
                agz(c)
    for b, i in bands[half_way:]:
        vert(1, b, i)
    for act in (agp, agc):
        for c in range(2, len(chunks)):
            act(c)
    finish()
    for c in range(2, len(chunks)):
        age(c)
    assert not flight
    for copy in pending:
        copy.wait_send()


def body(n_gx, n_gy, object_field, probe_field, amplitude, offsets):
    extent = probe_field.shape[-1]
    modes = probe_field.shape[0]
    margin = extent // 2
    rows, cols = object_field.shape[1:]
    positions = amplitude.shape[0]
    mt, ct = margin // LANE, cols // LANE
    ext_shape = (2, 2 * mt + ct, rows + 2 * margin, LANE)
    ext = pl.pallas_call(
        functools.partial(halo_kernel, n_gx, n_gy, margin),
        out_shape=jax.ShapeDtypeStruct(ext_shape, F32),
        in_specs=[HBM],
        out_specs=VMEM,
        scratch_shapes=[pltpu.SemaphoreType.DMA((2, (2 + 8 * STRIPS) * mt)), pltpu.SemaphoreType.DMA((ct,))],
        compiler_params=pltpu.CompilerParams(collective_id=0, has_side_effects=True, vmem_limit_bytes=LIMIT),
        name="halo",
    )(object_field)

    planes = 2 * modes + 1
    steps = len(reduce_plan(n_gx, n_gy, "x"))
    peers = max(
        sum((1 << (cx + cy)) - 1 for _, cx, _, cy in reduce_plan(n_gx, n_gy, kind)) for kind in "xy"
    )
    out_obj, out_probe = pl.pallas_call(
        functools.partial(step_kernel, n_gx, n_gy, margin),
        out_shape=(
            jax.ShapeDtypeStruct(object_field.shape, F32),
            jax.ShapeDtypeStruct((2 * modes, extent, extent), F32),
        ),
        in_specs=[pl.BlockSpec(memory_space=pltpu.SMEM)] + [VMEM] * 5,
        out_specs=(VMEM, VMEM),
        scratch_shapes=[
            pltpu.VMEM((positions, 2, extent, extent), F32),
            pltpu.VMEM((positions, modes, 2, extent, extent), F32),
            pltpu.VMEM((positions, 2 * extent, modes * extent), BF16),
            pltpu.VMEM((modes * extent, 2 * extent), BF16),
            pltpu.VMEM((2, modes * extent, 2 * extent), F32),
            pltpu.VMEM((2, extent, 2 * extent), BF16),
            pltpu.VMEM((2, extent, 2 * extent), F32),
            pltpu.VMEM((positions, 2, extent, extent), F32),
            pltpu.VMEM((2 * extent, 2 * extent), BF16),
            pltpu.VMEM((2 * extent, 2 * extent), BF16),
            pltpu.VMEM((positions, 2, extent // LANE + 1, extent + 2 * CHUNK, LANE), F32),
            pltpu.VMEM(ext_shape, F32),
            pltpu.VMEM((planes, extent, extent), F32),
            pltpu.VMEM((2, mt, rows + 2 * margin, LANE), F32),
            pltpu.VMEM((2, mt, rows + 2 * margin, LANE), F32),
            pltpu.VMEM((2, 2, 2, mt, margin, LANE), F32),
            pltpu.VMEM((2, 2, 2, mt, margin, LANE), F32),
            pltpu.VMEM((steps, planes + 1, extent, extent), F32),
            pltpu.VMEM((planes + 1, 2 * extent, extent), F32),
            pltpu.SemaphoreType.DMA((2, 8 * PIECES + 2 * MIDS + (peers + 24) * (modes + 2))),
        ],
        compiler_params=pltpu.CompilerParams(
            collective_id=1, has_side_effects=True, vmem_limit_bytes=STEP_LIMIT
        ),
        name="step",
    )(offsets.transpose(1, 2, 0), ext, object_field, probe_field, amplitude[:, 0], dft_tables(extent))
    return out_obj, out_probe.reshape(probe_field.shape)


def solution(mesh):
    in_specs = (P(None, "gx", "gy"), P(), P("gx", "gy", None, None), P("gx", "gy", None))
    out_specs = (P(None, "gx", "gy"), P())
    step = functools.partial(body, mesh.shape["gx"], mesh.shape["gy"])
    return jax.shard_map(step, mesh=mesh, in_specs=in_specs, out_specs=out_specs, check_vma=False)
```

```python
import functools
import math

import jax
import jax.numpy as jnp
import numpy as np
from jax import lax
from jax.experimental import pallas as pl
from jax.experimental.pallas import tpu as pltpu
from jax.sharding import PartitionSpec as P

MESH = pl.DeviceIdType.MESH
VMEM = pl.BlockSpec(memory_space=pltpu.VMEM)
HBM = pl.BlockSpec(memory_space=pltpu.MemorySpace.HBM)
F32 = jnp.float32
BF16 = jnp.bfloat16
CHUNK = 32
SUB = 8
LANE = 128
STRIPS = 2
PIECES = 2
MIDS = 2
LIMIT = 8 << 20
STEP_LIMIT = 40 << 20


def dft_tables(extent):
    indices = np.arange(extent)
    angles = (indices[:, None] * indices[None, :] % extent) * (2.0 * math.pi / extent)
    norm_factor = 1.0 / math.sqrt(extent)
    both = np.concatenate([np.cos(angles), np.sin(angles)], 1) * norm_factor
    return jnp.asarray(both.astype(np.float32).astype(jnp.bfloat16))


def remote(src, dst, sems, slot, device):
    return pltpu.make_async_remote_copy(
        src_ref=src,
        dst_ref=dst,
        send_sem=sems.at[0, slot],
        recv_sem=sems.at[1, slot],
        device_id=device,
        device_id_type=MESH,
    )


def greet(devices):
    barrier = pltpu.get_barrier_semaphore()
    for device in devices:
        pl.semaphore_signal(barrier, inc=1, device_id=device, device_id_type=MESH)
    pl.semaphore_wait(barrier, len(devices))


def halo_kernel(n_gx, n_gy, margin, obj, ext, sems, local_sem):
    gx, gy = lax.axis_index("gx"), lax.axis_index("gy")
    rows, cols = obj.shape[1], obj.shape[2]
    m = margin
    mt, ct = m // LANE, cols // LANE
    odd = lax.rem(gy, 2)
    up = (lax.rem(gx + n_gx - 1, n_gx), gy)
    down = (lax.rem(gx + 1, n_gx), gy)
    step_y = 1 - 2 * odd
    near = (gx, gy + step_y)
    far = (gx, lax.rem(gy - step_y + n_gy, n_gy))
    sides = (near, far)
    half_at = ((1 - odd) * (ct - mt), odd * (ct - mt))
    lands_at = (odd * (mt + ct), (1 - odd) * (mt + ct))
    owns = [
        pltpu.make_async_copy(
            obj.at[:, :, pl.ds(t * LANE, LANE)], ext.at[:, mt + t, pl.ds(m, rows), :], local_sem.at[t]
        )
        for t in range(ct)
    ]
    for own in owns:
        own.start()
    greet((up, down, near, far))
    slot = [0]
    pending = []

    def send(src, dst, device):
        copy = remote(src, dst, sems, slot[0], device)
        slot[0] += 1
        copy.start()
        pending.append(copy)
        return copy

    piece = m // STRIPS
    ways = ((0, m + rows, up), (rows - m, 0, down))
    arrivals = []
    waits = []

    def lanes(side, t):
        return pl.ds(pl.multiple_of((half_at[side] + t) * LANE, LANE), LANE)

    def middle(side):
        for t in range(mt):
            dst = ext.at[:, lands_at[side] + t, pl.ds(m, rows), :]
            waits.append(send(obj.at[:, :, lanes(side, t)], dst, sides[side]))

    def vertical(side):
        for i in range(STRIPS):
            for src_row, dst_row, device in ways:
                band = pl.ds(dst_row + i * piece, piece)
                for t in range(mt):
                    src = obj.at[:, pl.ds(src_row + i * piece, piece), lanes(side, t)]
                    dst = ext.at[:, mt + half_at[side] + t, band, :]
                    arrivals.append((send(src, dst, device), side, band, t))

    vertical(1)
    middle(1)
    vertical(0)
    middle(0)
    for copy, side, band, t in arrivals:
        copy.wait_recv()
        src = ext.at[:, mt + half_at[side] + t, band, :]
        waits.append(send(src, ext.at[:, lands_at[side] + t, band, :], sides[side]))
    for copy in waits:
        copy.wait_recv()
    for copy in pending:
        copy.wait_send()
    for own in owns:
        own.wait()


def reduce_plan(n_gx, n_gy):
    x_bits, y_bits = n_gx.bit_length() - 1, n_gy.bit_length() - 1
    steps = [(0, 0, 0, 1), (0, 1, 1, 1)]
    steps.append((1, min(2, x_bits - 1), 0, 0))
    for b in range(3, x_bits, 2):
        steps.append((b, min(2, x_bits - b), 0, 0))
    for b in range(2, y_bits, 2):
        steps.append((0, 0, b, min(2, y_bits - b)))
    return steps


def step_kernel(n_gx, n_gy, margin, offs, ext, probe, amp, table, out_obj, out_probe, *scratch):
    (win, psi, xbuf, ybuf, ffwd, yback, fback, half, fr, frt, pads, acc, sums) = scratch[:13]
    (from_near, from_far, vsend, vrecv, part, inbox, sems) = scratch[13:]
    positions = amp.shape[0]
    gx, gy = lax.axis_index("gx"), lax.axis_index("gy")
    rows, cols = out_obj.shape[1], out_obj.shape[2]
    planes, extent = sums.shape[0], sums.shape[1]
    modes = probe.shape[0]
    m = margin
    mt, ct = m // LANE, cols // LANE
    odd = lax.rem(gy, 2)
    up = (lax.rem(gx + n_gx - 1, n_gx), gy)
    down = (lax.rem(gx + 1, n_gx), gy)
    step_y = 1 - 2 * odd
    near = (gx, gy + step_y)
    far = (gx, lax.rem(gy - step_y + n_gy, n_gy))
    sides = (near, far)
    came = (from_near, from_far)
    halo_at = ((1 - odd) * (mt + ct), odd * (mt + ct))
    half_at = (mt + (1 - odd) * (ct - mt), mt + odd * (ct - mt))
    plan = reduce_plan(n_gx, n_gy)
    steps = len(plan)
    chunks = [(0, 1)] + [(2 * i + 1, 2 * i + 3) for i in range(modes)]

    def swap(field, d, bits):
        out = 0
        for b in range(bits):
            bit = lax.rem(field // (1 << b), 2)
            out = out + (1 << b) * (1 - bit if d >> b & 1 else bit)
        return out

    def members(bx, cx, by, cy):
        nx, ny = 1 << cx, 1 << cy
        fx, fy = lax.rem(gx // (1 << bx), nx), lax.rem(gy // (1 << by), ny)
        peers = []
        for dy in range(ny):
            for dx in range(nx):
                if dx or dy:
                    px, py = swap(fx, dx, cx), swap(fy, dy, cy)
                    peers.append((px + nx * py, (gx + (px - fx) * (1 << bx), gy + (py - fy) * (1 << by))))
        return nx * ny, fx + nx * fy, peers

    friends = [up, down, near, far] + [dev for g in plan for _, dev in members(*g)[2]]
    barrier = pltpu.get_barrier_semaphore()
    for device in friends:
        pl.semaphore_signal(barrier, inc=1, device_id=device, device_id_type=MESH)

    slot = [0]
    pending = []

    def send(src, dst, device):
        copy = remote(src, dst, sems, slot[0], device)
        slot[0] += 1
        copy.start()
        pending.append(copy)
        return copy

    state = [{"off": 0, "n": extent, "src": sums, "box": 0} for _ in chunks]
    history = [[] for _ in chunks]
    flight = {}

    def rws(at, n):
        return pl.ds(pl.multiple_of(at, SUB), n)

    def rs(step, c):
        lo, hi = chunks[c]
        s = state[c]
        size, mine, peers = members(*plan[step])
        split = step < 3
        n = s["n"] // size if split else s["n"]
        copies = []
        for field, device in peers:
            give = s["off"] + field * n if split else s["off"]
            box = s["box"] + mine * n
            copies.append(send(s["src"].at[lo:hi, rws(give, n), :], inbox.at[lo:hi, rws(box, n), :], device))
        keep = s["off"] + mine * n if split else s["off"]
        history[c].append((size, mine, peers, split))
        flight["rs", step, c] = (copies, keep, n, size, mine, [f for f, _ in peers], s["box"], split)
        s["box"] += size * n

    def rse(step, c):
        lo, hi = chunks[c]
        copies, keep, n, size, mine, fields, box, split = flight.pop(("rs", step, c))
        s = state[c]
        for copy in copies:
            copy.wait_recv()
        own = s["src"][lo:hi, rws(keep, n), :]
        if split:
            total = own
            for f in fields:
                total += inbox[lo:hi, rws(box + f * n, n), :]
        else:
            inbox[lo:hi, rws(box + mine * n, n), :] = own
            total = inbox[lo:hi, rws(box, n), :]
            for j in range(1, size):
                total += inbox[lo:hi, rws(box + j * n, n), :]
        part[step, lo:hi, rws(keep, n), :] = total
        s["off"], s["n"], s["src"] = keep, n, part.at[step]

    def div(c):
        lo, hi = chunks[c]
        first = 1 if lo == 0 else 0
        s = state[c]
        keep = rws(s["off"], s["n"])
        weight = s["src"][0, keep, :] + 1e-05
        for k in range(lo + first, hi):
            out_probe[k - 1, keep, :] = s["src"][k, keep, :] / weight

    def planes_of(c):
        lo, hi = chunks[c][:2]
        return max(lo - 1, 0), hi - 1

    def give(c, off, n, device):
        lo, hi = planes_of(c)
        own = out_probe.at[lo:hi, rws(off, n), :]
        return send(own, own, device)

    def agz(c):
        off, n = state[c]["off"], state[c]["n"]
        _, _, z_peers, _ = history[c][2]
        _, _, p_peers, _ = history[c][1]
        zs = [give(c, off, n, device) for _, device in z_peers]
        ps = [[give(c, off, n, device)] for _, device in p_peers]
        flight["agz", c] = (zs, ps)

    def agp(c):
        off, n = state[c]["off"], state[c]["n"]
        z_size, z_mine, z_peers, _ = history[c][2]
        _, _, p_peers, _ = history[c][1]
        _, _, ((_, partner),), _ = history[c][0]
        zs, ps = flight.pop(("agz", c))
        base = off - z_mine * n
        for (field, _), copy in zip(z_peers, zs):
            copy.wait_recv()
            for (_, device), got in zip(p_peers, ps):
                got.append(give(c, base + field * n, n, device))
        flight["agp", c] = (ps, base, n * z_size, [give(c, base, n * z_size, partner)])

    def agc(c):
        ps, base, n, cs = flight.pop(("agp", c))
        p_size, p_mine, p_peers, _ = history[c][1]
        _, _, ((_, partner),), _ = history[c][0]
        for (field, _), copies in zip(p_peers, ps):
            for copy in copies:
                copy.wait_recv()
            cs.append(give(c, base + (field - p_mine) * n, n, partner))
        flight["agc", c] = cs

    def age(c):
        for copy in flight.pop(("agc", c)):
            copy.wait_recv()

    band_at = (0, m + rows)
    piece = m // PIECES

    def corner(side, b, i):
        band = pl.ds(band_at[b] + i * piece, piece)
        flight["corner", side, b, i] = send(
            acc.at[:, pl.ds(halo_at[side], mt), band, :], came[side].at[:, :, band, :], sides[side]
        )

    def mid(side, i, of):
        band = pl.ds(m + i * (rows // of), rows // of)
        flight["mid", side, i] = send(
            acc.at[:, pl.ds(halo_at[side], mt), band, :], came[side].at[:, :, band, :], sides[side]
        )

    def vert(side, b, i):
        flight.pop(("corner", side, b, i)).wait_recv()
        band = pl.ds(band_at[b] + i * piece, piece)
        here = pl.ds(i * piece, piece)
        own = acc[:, pl.ds(half_at[side], mt), band, :]
        vsend[b, side, :, :, here, :] = own + came[side][:, :, band, :]
        flight["vert", side, b, i] = send(
            vsend.at[b, side, :, :, here, :], vrecv.at[b, side, :, :, here, :], (up, down)[b]
        )

    power_box = []
    def power():
        total = jnp.zeros((extent, extent), F32)
        for k in range(modes):
            for c in range(2):
                total += probe[k, c] * probe[k, c]
        power_box.append(jnp.max(total, keepdims=True) + 1e-06)

    def finish():
        scale = power_box[0]
        for key in [k for k in flight if k[0] in ("mid", "vert")]:
            flight.pop(key).wait_recv()
        for side in range(2):
            for t in range(mt):
                dst = pl.ds(pl.multiple_of((half_at[side] - mt + t) * LANE, LANE), LANE)
                for c in range(2):
                    base = acc[c, half_at[side] + t, pl.ds(m, rows), :] + came[side][c, t, pl.ds(m, rows), :]
                    ends = jnp.concatenate([vrecv[1, side, c, t], vrecv[0, side, c, t]], 0)
                    out_obj[c, :, dst] = (base + ends) / scale

    starts = range(0, extent, CHUNK)

    last = ext.shape[1] - extent // LANE - 1
    c, s = table[:, :extent], table[:, extent:]
    fr[:extent, :extent] = c
    fr[:extent, extent:] = s
    fr[extent:, :extent] = -s
    fr[extent:, extent:] = c
    frt[:extent, :extent] = c
    frt[:extent, extent:] = -s
    frt[extent:, :extent] = s
    frt[extent:, extent:] = c

    lane = lax.broadcasted_iota(jnp.int32, (CHUNK, LANE), 1)

    def place(p):
        c0 = offs[0, 1, p] + margin
        tile = jnp.minimum(c0 // LANE, last)
        return offs[0, 0, p] + margin, tile, c0 - tile * LANE

    def add(plane, here, value, p):
        if p == 0:
            sums[plane, here, :] = value
        else:
            sums[plane, here, :] += value

    def extract(p, rb):
        r0, tile, low = place(p)
        here = pl.ds(rb, CHUNK)
        w = []
        for c in range(2):
            line = [
                pltpu.roll(ext[c, tile + t, pl.ds(r0 + rb, CHUNK), :], lax.rem(LANE - low, LANE), 1)
                for t in range(extent // LANE + 1)
            ]
            line = [jnp.where(lane < LANE - low, a, b) for a, b in zip(line, line[1:])]
            w.append(jnp.concatenate(line, 1))
            win[p, c, here, :] = w[c]
        add(0, here, w[0] * w[0] + w[1] * w[1], p)
        for k in range(modes):
            cols = slice(k * extent, (k + 1) * extent)
            pr, pi = probe[k, 0, here, :], probe[k, 1, here, :]
            psi_re = pr * w[0] - pi * w[1]
            psi_im = pr * w[1] + pi * w[0]
            psi[p, k, 0, here, :] = psi_re
            psi[p, k, 1, here, :] = psi_im
            xbuf[p, here, cols] = psi_re.astype(BF16)
            xbuf[p, pl.ds(extent + rb, CHUNK), cols] = psi_im.astype(BF16)

    def rows_pass(p, c):
        band = fr[c * extent : (c + 1) * extent, :]
        out = jnp.dot(band, xbuf[p], preferred_element_type=F32).astype(BF16)
        for k in range(modes):
            ybuf[k * extent : (k + 1) * extent, c * extent : (c + 1) * extent] = out[
                :, k * extent : (k + 1) * extent
            ]

    def cols_pass(p, k):
        band = slice(k * extent, (k + 1) * extent)
        ffwd[p % 2, band, :] = jnp.dot(ybuf[band, :], frt[...], preferred_element_type=F32)

    def rows_back(k, p, c):
        band = frt[c * extent : (c + 1) * extent, :]
        cols = slice(k * extent, (k + 1) * extent)
        out = jnp.dot(band, xbuf[p, :, cols], preferred_element_type=F32)
        yback[p % 2, :, c * extent : (c + 1) * extent] = out.astype(BF16)

    def cols_back(k, p):
        fback[p % 2] = jnp.dot(yback[p % 2], fr[...], preferred_element_type=F32)

    def project(p, rb):
        q = p % 2
        parts = []
        intensity = jnp.zeros((CHUNK, extent), F32)
        for k in range(modes):
            at = pl.ds(k * extent + rb, CHUNK)
            re, im = ffwd[q, at, :extent], ffwd[q, at, extent:]
            intensity += re * re + im * im
            parts.append((re, im))
        factor = amp[p, pl.ds(rb, CHUNK), :] * jnp.minimum(lax.rsqrt(intensity), 4.0)
        for k in range(modes):
            cols = slice(k * extent, (k + 1) * extent)
            xbuf[p, pl.ds(rb, CHUNK), cols] = (parts[k][0] * factor).astype(BF16)
            xbuf[p, pl.ds(extent + rb, CHUNK), cols] = (parts[k][1] * factor).astype(BF16)

    def correct(k, p, rb):
        here = pl.ds(rb, CHUNK)
        wr, wi = win[p, 0, here, :], win[p, 1, here, :]
        dr = fback[p % 2, here, :extent] - psi[p, k, 0, here, :]
        di = fback[p % 2, here, extent:] - psi[p, k, 1, here, :]
        pr, pi = probe[k, 0, here, :], probe[k, 1, here, :]
        add(2 * k + 1, here, wr * dr + wi * di, p)
        add(2 * k + 2, here, wr * di - wi * dr, p)
        value = [pr * dr + pi * di, pr * di - pi * dr]
        if k:
            value = [half[p, c, here, :] + value[c] for c in range(2)]
        if k + 1 < modes:
            for c in range(2):
                half[p, c, here, :] = value[c]
            return
        _, _, low = place(p)
        blank = jnp.zeros((CHUNK, LANE), F32)
        for c in range(2):
            line = [
                pltpu.roll(value[c][:, t * LANE : (t + 1) * LANE], lax.rem(low, LANE), 1)
                for t in range(extent // LANE)
            ]
            for t, (a, b) in enumerate(zip([blank] + line, line + [blank])):
                pads[p, c, t, pl.ds(CHUNK + rb, CHUNK), :] = jnp.where(lane < low, a, b)

    def blank_pads(p):
        for at in (0, CHUNK + extent):
            pads[p, :, :, at : at + CHUNK, :] = jnp.zeros((2, pads.shape[2], CHUNK, LANE), F32)

    def gather(lo, hi):
        tiles = pads.shape[2]
        for at in range(lo, hi, CHUNK):
            for t in range(acc.shape[1]):
                spots = []
                for p in range(positions):
                    r0, tile, _ = place(p)
                    row = jnp.clip(at - r0, -CHUNK, extent) + CHUNK
                    inside = (t >= tile) & (t < tile + tiles)
                    spots.append((p, jnp.clip(t - tile, 0, tiles - 1), jnp.where(inside, row, 0)))
                for c in range(2):
                    total = None
                    for p, tile, row in spots:
                        value = pads[p, c, tile, pl.ds(row, CHUNK), :]
                        total = value if total is None else total + value
                    acc[c, t, at : at + CHUNK, :] = total

    def beside(matmuls, others):
        n = len(matmuls)
        for i, (call, args) in enumerate(matmuls):
            call(*args)
            for other, rest in others[i * len(others) // n : (i + 1) * len(others) // n]:
                other(*rest)

    for rb in starts:
        extract(0, rb)
    for p in range(positions):
        beside(
            [(rows_pass, (p, 0)), (rows_pass, (p, 1))] + [(cols_pass, (p, k)) for k in range(modes)],
            [(blank_pads, (p,))]
            + ([(project, (p - 1, rb)) for rb in starts] if p else [])
            + ([(extract, (p + 1, rb)) for rb in starts] if p + 1 < positions else []),
        )
    for rb in starts:
        project(positions - 1, rb)
    pl.semaphore_wait(barrier, len(friends))
    rs(0, 0)

    def back(k, p):
        return [(rows_back, (k, p, 0)), (rows_back, (k, p, 1)), (cols_back, (k, p))]

    n = len(chunks)
    units = [(k, p) for k in range(modes) for p in range(positions)]
    beside(back(*units[0]), [])
    for u, (k, p) in enumerate(units):
        rest = [(correct, (k, p, rb)) for rb in starts]
        if u + 1 < len(units):
            beside(back(*units[u + 1]), rest)
        else:
            for call, args in rest:
                call(*args)
        if u + 2 == len(units):
            for c in range(1, n - 1):
                rse(0, c)
                rs(1, c)
        if u == 2:
            rse(0, 0)
            rs(1, 0)
        if p + 1 == positions:
            rs(0, 1 + k)

    bands = [(b, i) for i in range(PIECES) for b in (0, 1)]

    def corners(side):
        for b, i in bands:
            corner(side, b, i)

    gather(0, m)
    gather(m + rows, m + rows + m)
    corners(0)
    rse(1, 0)
    rs(2, 0)
    rse(0, n - 1)
    rs(1, n - 1)
    corners(1)
    gather(m, m + rows)
    power()
    for b, i in bands:
        vert(0, b, i)
    for c in range(1, n):
        rse(1, c)
        rs(2, c)
    for side in (1, 0):
        for i in range(MIDS):
            mid(side, i, MIDS)
    for b, i in bands:
        vert(1, b, i)
    for s in range(2, steps):
        for c in range(n):
            rse(s, c)
            if s + 1 < steps:
                rs(s + 1, c)
            elif c:
                div(c)
                agz(c)
    for act in (agp, agc):
        for c in range(1, n):
            act(c)
    finish()
    for c in range(1, n):
        age(c)
    assert not flight
    for copy in pending:
        copy.wait_send()


def body(n_gx, n_gy, object_field, probe_field, amplitude, offsets):
    extent = probe_field.shape[-1]
    modes = probe_field.shape[0]
    margin = extent // 2
    rows, cols = object_field.shape[1:]
    positions = amplitude.shape[0]
    mt, ct = margin // LANE, cols // LANE
    ext_shape = (2, 2 * mt + ct, rows + 2 * margin, LANE)
    ext = pl.pallas_call(
        functools.partial(halo_kernel, n_gx, n_gy, margin),
        out_shape=jax.ShapeDtypeStruct(ext_shape, F32),
        in_specs=[HBM],
        out_specs=VMEM,
        scratch_shapes=[pltpu.SemaphoreType.DMA((2, (2 + 8 * STRIPS) * mt)), pltpu.SemaphoreType.DMA((ct,))],
        compiler_params=pltpu.CompilerParams(collective_id=0, has_side_effects=True, vmem_limit_bytes=LIMIT),
        name="halo",
    )(pltpu.with_memory_space_constraint(object_field, pltpu.MemorySpace.HBM))

    planes = 2 * modes + 1
    plan = reduce_plan(n_gx, n_gy)
    peers = sum((1 << (cx + cy)) - 1 for _, cx, _, cy in plan)
    out_obj, out_probe = pl.pallas_call(
        functools.partial(step_kernel, n_gx, n_gy, margin),
        out_shape=(
            jax.ShapeDtypeStruct(object_field.shape, F32),
            jax.ShapeDtypeStruct((2 * modes, extent, extent), F32),
        ),
        in_specs=[pl.BlockSpec(memory_space=pltpu.SMEM), VMEM, VMEM, VMEM, VMEM],
        out_specs=(VMEM, VMEM),
        scratch_shapes=[
            pltpu.VMEM((positions, 2, extent, extent), F32),
            pltpu.VMEM((positions, modes, 2, extent, extent), F32),
            pltpu.VMEM((positions, 2 * extent, modes * extent), BF16),
            pltpu.VMEM((modes * extent, 2 * extent), BF16),
            pltpu.VMEM((2, modes * extent, 2 * extent), F32),
            pltpu.VMEM((2, extent, 2 * extent), BF16),
            pltpu.VMEM((2, extent, 2 * extent), F32),
            pltpu.VMEM((positions, 2, extent, extent), F32),
            pltpu.VMEM((2 * extent, 2 * extent), BF16),
            pltpu.VMEM((2 * extent, 2 * extent), BF16),
            pltpu.VMEM((positions, 2, extent // LANE + 1, extent + 2 * CHUNK, LANE), F32),
            pltpu.VMEM(ext_shape, F32),
            pltpu.VMEM((planes, extent, extent), F32),
            pltpu.VMEM((2, mt, rows + 2 * margin, LANE), F32),
            pltpu.VMEM((2, mt, rows + 2 * margin, LANE), F32),
            pltpu.VMEM((2, 2, 2, mt, margin, LANE), F32),
            pltpu.VMEM((2, 2, 2, mt, margin, LANE), F32),
            pltpu.VMEM((len(plan), planes, extent, extent), F32),
            pltpu.VMEM((planes, 2 * extent, extent), F32),
            pltpu.SemaphoreType.DMA((2, 8 * PIECES + 2 * MIDS + (peers + 24) * (modes + 1))),
        ],
        compiler_params=pltpu.CompilerParams(
            collective_id=1, has_side_effects=True, vmem_limit_bytes=STEP_LIMIT
        ),
        name="step",
    )(offsets.transpose(1, 2, 0), ext, probe_field, amplitude[:, 0], dft_tables(extent))
    return object_field + out_obj, probe_field + out_probe.reshape(probe_field.shape)


def solution(mesh):
    in_specs = (P(None, "gx", "gy"), P(), P("gx", "gy", None, None), P("gx", "gy", None))
    out_specs = (P(None, "gx", "gy"), P())
    step = functools.partial(body, mesh.shape["gx"], mesh.shape["gy"])
    return jax.shard_map(step, mesh=mesh, in_specs=in_specs, out_specs=out_specs, check_vma=False)
```

```python
import functools
import math

import jax
import jax.numpy as jnp
import numpy as np
from jax import lax
from jax.experimental import pallas as pl
from jax.experimental.pallas import tpu as pltpu
from jax.sharding import PartitionSpec as P

MESH = pl.DeviceIdType.MESH
VMEM = pl.BlockSpec(memory_space=pltpu.VMEM)
HBM = pl.BlockSpec(memory_space=pltpu.MemorySpace.HBM)
ANY = pl.BlockSpec(memory_space=pl.ANY)
F32 = jnp.float32
BF16 = jnp.bfloat16
CHUNK = 32
SUB = 8
LANE = 128
STRIPS = 2
PIECES = 2
MIDS = 2
LIMIT = 8 << 20
STEP_LIMIT = 40 << 20
EMIT_LIMIT = 2 << 20


def dft_tables(extent):
    indices = np.arange(extent)
    angles = (indices[:, None] * indices[None, :] % extent) * (2.0 * math.pi / extent)
    norm_factor = 1.0 / math.sqrt(extent)
    both = np.concatenate([np.cos(angles), np.sin(angles)], 1) * norm_factor
    return jnp.asarray(both.astype(np.float32).astype(jnp.bfloat16))


def remote(src, dst, sems, slot, device):
    return pltpu.make_async_remote_copy(
        src_ref=src,
        dst_ref=dst,
        send_sem=sems.at[0, slot],
        recv_sem=sems.at[1, slot],
        device_id=device,
        device_id_type=MESH,
    )


def greet(devices):
    barrier = pltpu.get_barrier_semaphore()
    for device in devices:
        pl.semaphore_signal(barrier, inc=1, device_id=device, device_id_type=MESH)
    pl.semaphore_wait(barrier, len(devices))


def halo_kernel(n_gx, n_gy, margin, obj, ext, sems, local_sem):
    gx, gy = lax.axis_index("gx"), lax.axis_index("gy")
    rows, cols = obj.shape[1], obj.shape[2]
    m = margin
    mt, ct = m // LANE, cols // LANE
    odd = lax.rem(gy, 2)
    up = (lax.rem(gx + n_gx - 1, n_gx), gy)
    down = (lax.rem(gx + 1, n_gx), gy)
    step_y = 1 - 2 * odd
    near = (gx, gy + step_y)
    far = (gx, lax.rem(gy - step_y + n_gy, n_gy))
    sides = (near, far)
    half_at = ((1 - odd) * (ct - mt), odd * (ct - mt))
    lands_at = (odd * (mt + ct), (1 - odd) * (mt + ct))
    owns = [
        pltpu.make_async_copy(
            obj.at[:, :, pl.ds(t * LANE, LANE)], ext.at[:, mt + t, pl.ds(m, rows), :], local_sem.at[t]
        )
        for t in range(ct)
    ]
    for own in owns:
        own.start()
    greet((up, down, near, far))
    slot = [0]
    pending = []

    def send(src, dst, device):
        copy = remote(src, dst, sems, slot[0], device)
        slot[0] += 1
        copy.start()
        pending.append(copy)
        return copy

    piece = m // STRIPS
    ways = ((0, m + rows, up), (rows - m, 0, down))
    arrivals = []
    waits = []

    def lanes(side, t):
        return pl.ds(pl.multiple_of((half_at[side] + t) * LANE, LANE), LANE)

    def middle(side):
        for t in range(mt):
            dst = ext.at[:, lands_at[side] + t, pl.ds(m, rows), :]
            waits.append(send(obj.at[:, :, lanes(side, t)], dst, sides[side]))

    def vertical(side):
        for i in range(STRIPS):
            for src_row, dst_row, device in ways:
                band = pl.ds(dst_row + i * piece, piece)
                for t in range(mt):
                    src = obj.at[:, pl.ds(src_row + i * piece, piece), lanes(side, t)]
                    dst = ext.at[:, mt + half_at[side] + t, band, :]
                    arrivals.append((send(src, dst, device), side, band, t))

    vertical(1)
    middle(1)
    vertical(0)
    middle(0)
    for copy, side, band, t in arrivals:
        copy.wait_recv()
        src = ext.at[:, mt + half_at[side] + t, band, :]
        waits.append(send(src, ext.at[:, lands_at[side] + t, band, :], sides[side]))
    for copy in waits:
        copy.wait_recv()
    for copy in pending:
        copy.wait_send()
    for own in owns:
        own.wait()


def reduce_plan(n_gx, n_gy):
    x_bits, y_bits = n_gx.bit_length() - 1, n_gy.bit_length() - 1
    steps = [(0, 0, 0, 1), (0, 1, 1, 1)]
    steps.append((1, min(2, x_bits - 1), 0, 0))
    for b in range(3, x_bits, 2):
        steps.append((b, min(2, x_bits - b), 0, 0))
    for b in range(2, y_bits, 2):
        steps.append((0, 0, b, min(2, y_bits - b)))
    return steps


def step_kernel(n_gx, n_gy, margin, offs, ext, probe, amp, table, out_obj, out_probe, *scratch):
    (win, psi, xbuf, ybuf, ffwd, yback, fback, half, fr, frt, pads, acc, sums) = scratch[:13]
    (from_near, from_far, vsend, vrecv, part, inbox, sems) = scratch[13:]
    positions = amp.shape[0]
    gx, gy = lax.axis_index("gx"), lax.axis_index("gy")
    rows, cols = out_obj.shape[1], out_obj.shape[2]
    planes, extent = sums.shape[0], sums.shape[1]
    modes = probe.shape[0]
    m = margin
    mt, ct = m // LANE, cols // LANE
    odd = lax.rem(gy, 2)
    up = (lax.rem(gx + n_gx - 1, n_gx), gy)
    down = (lax.rem(gx + 1, n_gx), gy)
    step_y = 1 - 2 * odd
    near = (gx, gy + step_y)
    far = (gx, lax.rem(gy - step_y + n_gy, n_gy))
    sides = (near, far)
    came = (from_near, from_far)
    halo_at = ((1 - odd) * (mt + ct), odd * (mt + ct))
    half_at = (mt + (1 - odd) * (ct - mt), mt + odd * (ct - mt))
    plan = reduce_plan(n_gx, n_gy)
    steps = len(plan)
    chunks = [(0, 1)] + [(2 * i + 1, 2 * i + 3) for i in range(modes)]

    def swap(field, d, bits):
        out = 0
        for b in range(bits):
            bit = lax.rem(field // (1 << b), 2)
            out = out + (1 << b) * (1 - bit if d >> b & 1 else bit)
        return out

    def members(bx, cx, by, cy):
        nx, ny = 1 << cx, 1 << cy
        fx, fy = lax.rem(gx // (1 << bx), nx), lax.rem(gy // (1 << by), ny)
        peers = []
        for dy in range(ny):
            for dx in range(nx):
                if dx or dy:
                    px, py = swap(fx, dx, cx), swap(fy, dy, cy)
                    peers.append((px + nx * py, (gx + (px - fx) * (1 << bx), gy + (py - fy) * (1 << by))))
        return nx * ny, fx + nx * fy, peers

    friends = [up, down, near, far] + [dev for g in plan for _, dev in members(*g)[2]]
    barrier = pltpu.get_barrier_semaphore()
    for device in friends:
        pl.semaphore_signal(barrier, inc=1, device_id=device, device_id_type=MESH)

    slot = [0]
    pending = []

    def send(src, dst, device):
        copy = remote(src, dst, sems, slot[0], device)
        slot[0] += 1
        copy.start()
        pending.append(copy)
        return copy

    state = [{"off": 0, "n": extent, "src": sums, "box": 0} for _ in chunks]
    history = [[] for _ in chunks]
    flight = {}

    def rws(at, n):
        return pl.ds(pl.multiple_of(at, SUB), n)

    def rs(step, c):
        lo, hi = chunks[c]
        s = state[c]
        size, mine, peers = members(*plan[step])
        split = step < 3
        n = s["n"] // size if split else s["n"]
        copies = []
        for field, device in peers:
            give = s["off"] + field * n if split else s["off"]
            box = s["box"] + mine * n
            copies.append(send(s["src"].at[lo:hi, rws(give, n), :], inbox.at[lo:hi, rws(box, n), :], device))
        keep = s["off"] + mine * n if split else s["off"]
        history[c].append((size, mine, peers, split))
        flight["rs", step, c] = (copies, keep, n, size, mine, [f for f, _ in peers], s["box"], split)
        s["box"] += size * n

    def rse(step, c):
        lo, hi = chunks[c]
        copies, keep, n, size, mine, fields, box, split = flight.pop(("rs", step, c))
        s = state[c]
        for copy in copies:
            copy.wait_recv()
        own = s["src"][lo:hi, rws(keep, n), :]
        if split:
            total = own
            for f in fields:
                total += inbox[lo:hi, rws(box + f * n, n), :]
        else:
            inbox[lo:hi, rws(box + mine * n, n), :] = own
            total = inbox[lo:hi, rws(box, n), :]
            for j in range(1, size):
                total += inbox[lo:hi, rws(box + j * n, n), :]
        part[step, lo:hi, rws(keep, n), :] = total
        s["off"], s["n"], s["src"] = keep, n, part.at[step]

    def div(c):
        lo, hi = chunks[c]
        first = 1 if lo == 0 else 0
        s = state[c]
        keep = rws(s["off"], s["n"])
        weight = s["src"][0, keep, :] + 1e-05
        for k in range(lo + first, hi):
            mode, c = divmod(k - 1, 2)
            out_probe[k - 1, keep, :] = probe[mode, c, keep, :] + s["src"][k, keep, :] / weight

    def planes_of(c):
        lo, hi = chunks[c][:2]
        return max(lo - 1, 0), hi - 1

    def give(c, off, n, device):
        lo, hi = planes_of(c)
        own = out_probe.at[lo:hi, rws(off, n), :]
        return send(own, own, device)

    def agz(c):
        off, n = state[c]["off"], state[c]["n"]
        _, _, z_peers, _ = history[c][2]
        _, _, p_peers, _ = history[c][1]
        zs = [give(c, off, n, device) for _, device in z_peers]
        ps = [[give(c, off, n, device)] for _, device in p_peers]
        flight["agz", c] = (zs, ps)

    def agp(c):
        off, n = state[c]["off"], state[c]["n"]
        z_size, z_mine, z_peers, _ = history[c][2]
        _, _, p_peers, _ = history[c][1]
        _, _, ((_, partner),), _ = history[c][0]
        zs, ps = flight.pop(("agz", c))
        base = off - z_mine * n
        for (field, _), copy in zip(z_peers, zs):
            copy.wait_recv()
            for (_, device), got in zip(p_peers, ps):
                got.append(give(c, base + field * n, n, device))
        flight["agp", c] = (ps, base, n * z_size, [give(c, base, n * z_size, partner)])

    def agc(c):
        ps, base, n, cs = flight.pop(("agp", c))
        p_size, p_mine, p_peers, _ = history[c][1]
        _, _, ((_, partner),), _ = history[c][0]
        for (field, _), copies in zip(p_peers, ps):
            for copy in copies:
                copy.wait_recv()
            cs.append(give(c, base + (field - p_mine) * n, n, partner))
        flight["agc", c] = cs

    def age(c):
        for copy in flight.pop(("agc", c)):
            copy.wait_recv()

    band_at = (0, m + rows)
    piece = m // PIECES

    def corner(side, b, i):
        band = pl.ds(band_at[b] + i * piece, piece)
        flight["corner", side, b, i] = send(
            acc.at[:, pl.ds(halo_at[side], mt), band, :], came[side].at[:, :, band, :], sides[side]
        )

    def mid(side, i, of):
        band = pl.ds(m + i * (rows // of), rows // of)
        flight["mid", side, i] = send(
            acc.at[:, pl.ds(halo_at[side], mt), band, :], came[side].at[:, :, band, :], sides[side]
        )

    def vert(side, b, i):
        flight.pop(("corner", side, b, i)).wait_recv()
        band = pl.ds(band_at[b] + i * piece, piece)
        here = pl.ds(i * piece, piece)
        own = acc[:, pl.ds(half_at[side], mt), band, :]
        vsend[b, side, :, :, here, :] = own + came[side][:, :, band, :]
        flight["vert", side, b, i] = send(
            vsend.at[b, side, :, :, here, :], vrecv.at[b, side, :, :, here, :], (up, down)[b]
        )

    power_box = []
    def power():
        total = jnp.zeros((extent, extent), F32)
        for k in range(modes):
            for c in range(2):
                total += probe[k, c] * probe[k, c]
        power_box.append(jnp.max(total, keepdims=True) + 1e-06)

    def finish():
        scale = power_box[0]
        for key in [k for k in flight if k[0] in ("mid", "vert")]:
            flight.pop(key).wait_recv()
        for side in range(2):
            for t in range(mt):
                dst = pl.ds(pl.multiple_of((half_at[side] - mt + t) * LANE, LANE), LANE)
                for c in range(2):
                    base = acc[c, half_at[side] + t, pl.ds(m, rows), :] + came[side][c, t, pl.ds(m, rows), :]
                    ends = jnp.concatenate([vrecv[1, side, c, t], vrecv[0, side, c, t]], 0)
                    out_obj[c, :, dst] = (base + ends) / scale

    starts = range(0, extent, CHUNK)

    last = ext.shape[1] - extent // LANE - 1
    c, s = table[:, :extent], table[:, extent:]
    fr[:extent, :extent] = c
    fr[:extent, extent:] = s
    fr[extent:, :extent] = -s
    fr[extent:, extent:] = c
    frt[:extent, :extent] = c
    frt[:extent, extent:] = -s
    frt[extent:, :extent] = s
    frt[extent:, extent:] = c

    lane = lax.broadcasted_iota(jnp.int32, (CHUNK, LANE), 1)

    def place(p):
        c0 = offs[0, 1, p] + margin
        tile = jnp.minimum(c0 // LANE, last)
        return offs[0, 0, p] + margin, tile, c0 - tile * LANE

    def add(plane, here, value, p):
        if p == 0:
            sums[plane, here, :] = value
        else:
            sums[plane, here, :] += value

    def extract(p, rb):
        r0, tile, low = place(p)
        here = pl.ds(rb, CHUNK)
        w = []
        for c in range(2):
            line = [
                pltpu.roll(ext[c, tile + t, pl.ds(r0 + rb, CHUNK), :], lax.rem(LANE - low, LANE), 1)
                for t in range(extent // LANE + 1)
            ]
            line = [jnp.where(lane < LANE - low, a, b) for a, b in zip(line, line[1:])]
            w.append(jnp.concatenate(line, 1))
            win[p, c, here, :] = w[c]
        add(0, here, w[0] * w[0] + w[1] * w[1], p)
        for k in range(modes):
            cols = slice(k * extent, (k + 1) * extent)
            pr, pi = probe[k, 0, here, :], probe[k, 1, here, :]
            psi_re = pr * w[0] - pi * w[1]
            psi_im = pr * w[1] + pi * w[0]
            psi[p, k, 0, here, :] = psi_re
            psi[p, k, 1, here, :] = psi_im
            xbuf[p, here, cols] = psi_re.astype(BF16)
            xbuf[p, pl.ds(extent + rb, CHUNK), cols] = psi_im.astype(BF16)

    def rows_pass(p, c):
        band = fr[c * extent : (c + 1) * extent, :]
        out = jnp.dot(band, xbuf[p], preferred_element_type=F32).astype(BF16)
        for k in range(modes):
            ybuf[k * extent : (k + 1) * extent, c * extent : (c + 1) * extent] = out[
                :, k * extent : (k + 1) * extent
            ]

    def cols_pass(p, k):
        band = slice(k * extent, (k + 1) * extent)
        ffwd[p % 2, band, :] = jnp.dot(ybuf[band, :], frt[...], preferred_element_type=F32)

    def rows_back(k, p, c):
        band = frt[c * extent : (c + 1) * extent, :]
        cols = slice(k * extent, (k + 1) * extent)
        out = jnp.dot(band, xbuf[p, :, cols], preferred_element_type=F32)
        yback[p % 2, :, c * extent : (c + 1) * extent] = out.astype(BF16)

    def cols_back(k, p):
        fback[p % 2] = jnp.dot(yback[p % 2], fr[...], preferred_element_type=F32)

    def project(p, rb):
        q = p % 2
        parts = []
        intensity = jnp.zeros((CHUNK, extent), F32)
        for k in range(modes):
            at = pl.ds(k * extent + rb, CHUNK)
            re, im = ffwd[q, at, :extent], ffwd[q, at, extent:]
            intensity += re * re + im * im
            parts.append((re, im))
        factor = amp[p, pl.ds(rb, CHUNK), :] * jnp.minimum(lax.rsqrt(intensity), 4.0)
        for k in range(modes):
            cols = slice(k * extent, (k + 1) * extent)
            xbuf[p, pl.ds(rb, CHUNK), cols] = (parts[k][0] * factor).astype(BF16)
            xbuf[p, pl.ds(extent + rb, CHUNK), cols] = (parts[k][1] * factor).astype(BF16)

    def correct(k, p, rb):
        here = pl.ds(rb, CHUNK)
        wr, wi = win[p, 0, here, :], win[p, 1, here, :]
        dr = fback[p % 2, here, :extent] - psi[p, k, 0, here, :]
        di = fback[p % 2, here, extent:] - psi[p, k, 1, here, :]
        pr, pi = probe[k, 0, here, :], probe[k, 1, here, :]
        add(2 * k + 1, here, wr * dr + wi * di, p)
        add(2 * k + 2, here, wr * di - wi * dr, p)
        value = [pr * dr + pi * di, pr * di - pi * dr]
        if k:
            value = [half[p, c, here, :] + value[c] for c in range(2)]
        if k + 1 < modes:
            for c in range(2):
                half[p, c, here, :] = value[c]
            return
        _, _, low = place(p)
        blank = jnp.zeros((CHUNK, LANE), F32)
        for c in range(2):
            line = [
                pltpu.roll(value[c][:, t * LANE : (t + 1) * LANE], lax.rem(low, LANE), 1)
                for t in range(extent // LANE)
            ]
            for t, (a, b) in enumerate(zip([blank] + line, line + [blank])):
                pads[p, c, t, pl.ds(CHUNK + rb, CHUNK), :] = jnp.where(lane < low, a, b)

    def blank_pads(p):
        for at in (0, CHUNK + extent):
            pads[p, :, :, at : at + CHUNK, :] = jnp.zeros((2, pads.shape[2], CHUNK, LANE), F32)

    def gather(lo, hi):
        tiles = pads.shape[2]
        for at in range(lo, hi, CHUNK):
            for t in range(acc.shape[1]):
                spots = []
                for p in range(positions):
                    r0, tile, _ = place(p)
                    row = jnp.clip(at - r0, -CHUNK, extent) + CHUNK
                    inside = (t >= tile) & (t < tile + tiles)
                    spots.append((p, jnp.clip(t - tile, 0, tiles - 1), jnp.where(inside, row, 0)))
                for c in range(2):
                    total = None
                    for p, tile, row in spots:
                        value = pads[p, c, tile, pl.ds(row, CHUNK), :]
                        total = value if total is None else total + value
                    acc[c, t, at : at + CHUNK, :] = total

    def beside(matmuls, others):
        n = len(matmuls)
        for i, (call, args) in enumerate(matmuls):
            call(*args)
            for other, rest in others[i * len(others) // n : (i + 1) * len(others) // n]:
                other(*rest)

    for rb in starts:
        extract(0, rb)
    for p in range(positions):
        beside(
            [(rows_pass, (p, 0)), (rows_pass, (p, 1))] + [(cols_pass, (p, k)) for k in range(modes)],
            [(blank_pads, (p,))]
            + ([(project, (p - 1, rb)) for rb in starts] if p else [])
            + ([(extract, (p + 1, rb)) for rb in starts] if p + 1 < positions else []),
        )
    for rb in starts:
        project(positions - 1, rb)
    pl.semaphore_wait(barrier, len(friends))
    rs(0, 0)

    def back(k, p):
        return [(rows_back, (k, p, 0)), (rows_back, (k, p, 1)), (cols_back, (k, p))]

    n = len(chunks)
    units = [(k, p) for k in range(modes) for p in range(positions)]
    beside(back(*units[0]), [])
    for u, (k, p) in enumerate(units):
        rest = [(correct, (k, p, rb)) for rb in starts]
        if u + 1 < len(units):
            beside(back(*units[u + 1]), rest)
        else:
            for call, args in rest:
                call(*args)
        if u + 2 == len(units):
            for c in range(1, n - 1):
                rse(0, c)
                rs(1, c)
        if u == 2:
            rse(0, 0)
            rs(1, 0)
        if p + 1 == positions:
            rs(0, 1 + k)

    bands = [(b, i) for i in range(PIECES) for b in (0, 1)]

    def corners(side):
        for b, i in bands:
            corner(side, b, i)

    gather(0, m)
    gather(m + rows, m + rows + m)
    corners(0)
    rse(1, 0)
    rs(2, 0)
    rse(0, n - 1)
    rs(1, n - 1)
    corners(1)
    gather(m, m + rows)
    power()
    for b, i in bands:
        vert(0, b, i)
    for c in range(1, n):
        rse(1, c)
        rs(2, c)
    for side in (1, 0):
        for i in range(MIDS):
            mid(side, i, MIDS)
    for b, i in bands:
        vert(1, b, i)
    for s in range(2, steps):
        for c in range(n):
            rse(s, c)
            if s + 1 < steps:
                rs(s + 1, c)
            elif c:
                div(c)
                agz(c)
    for act in (agp, agc):
        for c in range(1, n):
            act(c)
    finish()
    for c in range(1, n):
        age(c)
    assert not flight
    for copy in pending:
        copy.wait_send()


def emit_kernel(obj, obj_step, probe, new_obj, new_probe, total, sems):
    probe_out = pltpu.make_async_copy(probe, new_probe, sems.at[0])
    probe_out.start()
    total[...] = obj[...] + obj_step[...]
    obj_out = pltpu.make_async_copy(total, new_obj, sems.at[1])
    obj_out.start()
    probe_out.wait()
    obj_out.wait()


def body(n_gx, n_gy, object_field, probe_field, amplitude, offsets):
    extent = probe_field.shape[-1]
    modes = probe_field.shape[0]
    margin = extent // 2
    rows, cols = object_field.shape[1:]
    positions = amplitude.shape[0]
    mt, ct = margin // LANE, cols // LANE
    ext_shape = (2, 2 * mt + ct, rows + 2 * margin, LANE)
    ext = pl.pallas_call(
        functools.partial(halo_kernel, n_gx, n_gy, margin),
        out_shape=jax.ShapeDtypeStruct(ext_shape, F32),
        in_specs=[HBM],
        out_specs=VMEM,
        scratch_shapes=[pltpu.SemaphoreType.DMA((2, (2 + 8 * STRIPS) * mt)), pltpu.SemaphoreType.DMA((ct,))],
        compiler_params=pltpu.CompilerParams(collective_id=0, has_side_effects=True, vmem_limit_bytes=LIMIT),
        name="halo",
    )(pltpu.with_memory_space_constraint(object_field, pltpu.MemorySpace.HBM))

    planes = 2 * modes + 1
    plan = reduce_plan(n_gx, n_gy)
    peers = sum((1 << (cx + cy)) - 1 for _, cx, _, cy in plan)
    out_obj, out_probe = pl.pallas_call(
        functools.partial(step_kernel, n_gx, n_gy, margin),
        out_shape=(
            jax.ShapeDtypeStruct(object_field.shape, F32),
            jax.ShapeDtypeStruct((2 * modes, extent, extent), F32),
        ),
        in_specs=[pl.BlockSpec(memory_space=pltpu.SMEM), VMEM, VMEM, VMEM, VMEM],
        out_specs=(VMEM, VMEM),
        scratch_shapes=[
            pltpu.VMEM((positions, 2, extent, extent), F32),
            pltpu.VMEM((positions, modes, 2, extent, extent), F32),
            pltpu.VMEM((positions, 2 * extent, modes * extent), BF16),
            pltpu.VMEM((modes * extent, 2 * extent), BF16),
            pltpu.VMEM((2, modes * extent, 2 * extent), F32),
            pltpu.VMEM((2, extent, 2 * extent), BF16),
            pltpu.VMEM((2, extent, 2 * extent), F32),
            pltpu.VMEM((positions, 2, extent, extent), F32),
            pltpu.VMEM((2 * extent, 2 * extent), BF16),
            pltpu.VMEM((2 * extent, 2 * extent), BF16),
            pltpu.VMEM((positions, 2, extent // LANE + 1, extent + 2 * CHUNK, LANE), F32),
            pltpu.VMEM(ext_shape, F32),
            pltpu.VMEM((planes, extent, extent), F32),
            pltpu.VMEM((2, mt, rows + 2 * margin, LANE), F32),
            pltpu.VMEM((2, mt, rows + 2 * margin, LANE), F32),
            pltpu.VMEM((2, 2, 2, mt, margin, LANE), F32),
            pltpu.VMEM((2, 2, 2, mt, margin, LANE), F32),
            pltpu.VMEM((len(plan), planes, extent, extent), F32),
            pltpu.VMEM((planes, 2 * extent, extent), F32),
            pltpu.SemaphoreType.DMA((2, 8 * PIECES + 2 * MIDS + (peers + 24) * (modes + 1))),
        ],
        compiler_params=pltpu.CompilerParams(
            collective_id=1, has_side_effects=True, vmem_limit_bytes=STEP_LIMIT
        ),
        name="step",
    )(offsets.transpose(1, 2, 0), ext, probe_field, amplitude[:, 0], dft_tables(extent))
    new_obj, new_probe = pl.pallas_call(
        emit_kernel,
        out_shape=(
            jax.ShapeDtypeStruct(object_field.shape, F32),
            jax.ShapeDtypeStruct(out_probe.shape, F32),
        ),
        in_specs=[VMEM] * 3,
        out_specs=(ANY, ANY),
        scratch_shapes=[pltpu.VMEM(object_field.shape, F32), pltpu.SemaphoreType.DMA((2,))],
        compiler_params=pltpu.CompilerParams(vmem_limit_bytes=EMIT_LIMIT),
        name="emit",
    )(object_field, out_obj, out_probe)
    return new_obj, new_probe.reshape(probe_field.shape)


def solution(mesh):
    in_specs = (P(None, "gx", "gy"), P(), P("gx", "gy", None, None), P("gx", "gy", None))
    out_specs = (P(None, "gx", "gy"), P())
    step = functools.partial(body, mesh.shape["gx"], mesh.shape["gy"])
    return jax.shard_map(step, mesh=mesh, in_specs=in_specs, out_specs=out_specs, check_vma=False)
```
